512 devices in a mesh: island: 16 (over z), fsdp: 32 (over x, y, core).
Axes of the slice: x: 4, y: 4, z: 16, core: 2. Of those that a mesh axis runs over, the one named last changes fastest.
Arguments:
- activations: bfloat16 [16, 11776, 4096], P('island', 'fsdp'), may hold values from -6 to 6
- key_grad: bfloat16 [16, 11776, 512], P('island', 'fsdp'), may hold values from -0.0546875 to 0.0546875
- island_weight: float32 [16, 4096, 512], P('island', 'fsdp'), may hold values from -0.09375 to 0.09375
- adam_m: float32 [16, 4096, 512], P('island', 'fsdp'), may hold values from -6 to 6
- adam_v: float32 [16, 4096, 512], P('island', 'fsdp'), may hold values from 0.2 to 2
- anchor: float32 [16, 256, 512], P('island', 'fsdp'), may hold values from -0.09375 to 0.09375
- outer_momentum: float32 [16, 256, 512], P('island', 'fsdp'), may hold values from -0.09375 to 0.09375
Outputs:
- adam_m_next: float32 [16, 4096, 512], P('island', 'fsdp')
- adam_v_next: float32 [16, 4096, 512], P('island', 'fsdp')
- island_weight_next: float32 [4096, 512], P('fsdp')
- anchor_next: float32 [16, 256, 512], P('island', 'fsdp')
- momentum_next: float32 [16, 256, 512], P('island', 'fsdp')
The draws below stay inside these ranges and needn't reach their ends.
All inputs are finite; a program needn't handle non-finite values.
Results may differ from the reference program's by a relative error of at most 0.0003.
Values may be sent and summed in bfloat16 or wider, within the bound.
A program may use at most 64 MiB of HBM per device.

```python
import math
import jax
import jax.numpy as jnp
from jax import lax

DW = 4096
KW = 512
ISLANDS = 16
TOKENS = 11776
SHARE = 8
N_FSDP = 32


def strengthened(result, own_key, source, target, parts, factor):
    owner, partner = [(jnp.arange(result.shape[position]) // (result.shape[position] // parts)).reshape([-1 if axis == position else 1 for axis in range(result.ndim)]) for position in (source, target)]
    chosen = jax.random.permutation(own_key, parts)[partner]
    strong = (owner == chosen) | (owner == (partner + parts // 2) % parts)
    return jnp.where(strong, factor * result, result)


def shard_levels(own_key, dims, split, low, top_value):
    def one(dim, parts):
        steps = jax.random.uniform(jax.random.fold_in(jax.random.fold_in(own_key, 6), dim), (parts,), jnp.float32, low / len(split), top_value / len(split))
        return jnp.repeat(jnp.exp(steps), dims[dim] // parts).reshape((-1,) + (1,) * (len(dims) - dim - 1))

    level = one(*split[0])
    for cut in split[1:]:
        level = level * one(*cut)
    return level


def gaussian(own_key, dims, scale, reach, cuts=(), kind=jnp.bfloat16):
    values = scale * jax.random.normal(own_key, dims, jnp.float32)
    if cuts:
        values = values * shard_levels(own_key, dims, cuts, -0.22, 0.18)
    return jnp.clip(values, -reach, reach).astype(kind)


def gaussian_with(key, shape, width, bound, cuts, heavy, kind=jnp.bfloat16):
    array = width * jax.random.normal(key, shape, jnp.float32)
    if cuts:
        array = array * shard_levels(key, shape, cuts, -0.22, 0.18)
    return jnp.clip(strengthened(array, jax.random.fold_in(key, 3), *heavy), -bound, bound).astype(kind)


def setup_inputs(seed: int = 0) -> dict:
    arg_keys = jax.random.split(jax.random.key(seed), 8)
    activations = gaussian_with(arg_keys[0], (ISLANDS, TOKENS, DW), 1.0, 6.0, ((0, 16), (1, 32)), (1, 2, 32, 2.75))
    key_grad = gaussian(arg_keys[1], (ISLANDS, TOKENS, KW), TOKENS ** -0.5, 0.0546875, ((0, 16), (1, 32)))
    island_weight = gaussian(arg_keys[2], (ISLANDS, DW, KW), DW ** -0.5, 0.09375, ((0, 16), (1, 32)), jnp.float32)
    adam_m = gaussian(arg_keys[3], (ISLANDS, DW, KW), 1.0, 6.0, ((0, 16), (1, 32)), jnp.float32)
    adam_v = jnp.clip(jnp.exp(math.log(2.0) - 2.3025851 * jax.random.uniform(arg_keys[4], (ISLANDS, DW, KW), jnp.float32) ** shard_levels(arg_keys[4], (ISLANDS, DW, KW), ((0, 16), (1, 32)), -0.2, 0.2)), 0.2, 2.0)
    anchor = gaussian(arg_keys[5], (ISLANDS, DW // ISLANDS, KW), DW ** -0.5, 0.09375, ((0, 16), (1, 32)), jnp.float32)
    outer_momentum = gaussian(arg_keys[6], (ISLANDS, DW // ISLANDS, KW), DW ** -0.5, 0.09375, ((0, 16), (1, 32)), jnp.float32)
    return {"activations": activations, "key_grad": key_grad, "island_weight": island_weight, "adam_m": adam_m, "adam_v": adam_v, "anchor": anchor, "outer_momentum": outer_momentum}


beta_first = 0.9
beta_second = 0.95
epsilon = 1e-08
inner_rate = 0.0004
decay_rate = 0.1
outer_beta = 0.9
outer_rate = 0.7

def to_matrix(blocks):
    return blocks.reshape(ISLANDS, N_FSDP, SHARE, KW).transpose(1, 0, 2, 3).reshape(DW, KW)

def from_matrix(matrix):
    return matrix.reshape(N_FSDP, ISLANDS, SHARE, KW).transpose(1, 0, 2, 3).reshape(ISLANDS, DW // ISLANDS, KW)

def island_grad(pair):
    return jnp.dot(pair[0].T, pair[1], preferred_element_type=jnp.float32)

def reference(activations, key_grad, island_weight, adam_m, adam_v, anchor, outer_momentum):
    grad = lax.map(island_grad, (activations, key_grad))
    m_next = beta_first * adam_m + (1.0 - beta_first) * grad
    v_next = beta_second * adam_v + (1.0 - beta_second) * grad * grad
    stepped = island_weight - inner_rate * (m_next / (jnp.sqrt(v_next) + epsilon) + decay_rate * island_weight)
    anchor_matrix = to_matrix(anchor)
    momentum_matrix = to_matrix(outer_momentum)
    shift = anchor_matrix - lax.optimization_barrier(jnp.sum(stepped, axis=0)) / ISLANDS
    moment = outer_beta * momentum_matrix + shift
    new_anchor = anchor_matrix - outer_rate * (shift + outer_beta * moment)
    return (m_next, v_next, new_anchor, from_matrix(new_anchor), from_matrix(moment))
```

```python
import jax
import jax.numpy as jnp
from jax import lax
from jax.experimental import pallas as pl
from jax.experimental.pallas import tpu as pltpu
from jax.sharding import PartitionSpec as P

beta_first = 0.9
beta_second = 0.95
epsilon = 1e-08
inner_rate = 0.0004
decay_rate = 0.1
outer_beta = 0.9
outer_rate = 0.7

SIDE = 4
STAGES = 4
MESH = pl.DeviceIdType.MESH


def window(
    islands,
    act, kg, weight, adam_m, adam_v, anchor, momentum,
    m_out, v_out, w_out, a_out, o_out,
    actb, kgb, part, got1, got2, wb, mb, vb, mnb, vnb, step_b, zgot, ab, ob, anb, onb,
    load_sem, act_sem, sib_send, sib_recv, xy_send, xy_recv, zr_send, zr_recv, ag_send, ag_recv, out_sem,
):
    me = lax.axis_index("island")
    flat = lax.axis_index("fsdp")
    core = lax.rem(flat, 2)
    chip = lax.div(flat, 2)
    x = lax.div(chip, SIDE)
    y = lax.rem(chip, SIDE)
    tokens = kg.shape[0]
    groups = islands // STAGES
    half_cols = kgb.shape[1] // 2
    sibling = flat + 1 - 2 * core

    def wrap(p):
        return lax.rem(p + 2 * SIDE, SIDE)

    def device(px, py):
        return (px * SIDE + py) * 2 + core

    loads = [
        pltpu.make_async_copy(kg, kgb.at[pl.ds(0, tokens)], load_sem.at[0]),
        pltpu.make_async_copy(weight, wb, load_sem.at[1]),
        pltpu.make_async_copy(adam_m, mb, load_sem.at[2]),
        pltpu.make_async_copy(adam_v, vb, load_sem.at[3]),
        pltpu.make_async_copy(anchor, ab, load_sem.at[4]),
        pltpu.make_async_copy(momentum, ob, load_sem.at[5]),
    ]

    def own_block(k):
        start = pl.multiple_of((2 * k + core) * 128, 128)
        return pltpu.make_async_copy(
            act.at[:, pl.ds(start, 128)], actb.at[k, pl.ds(0, tokens)], act_sem.at[k]
        )

    def sibling_block(k):
        start = pl.multiple_of((2 * k + 1 - core) * 128, 128)
        return pltpu.make_async_remote_copy(
            src_ref=act.at[:, pl.ds(start, 128)],
            dst_ref=actb.at[k, pl.ds(tokens, tokens)],
            send_sem=sib_send.at[k],
            recv_sem=sib_recv.at[k],
            device_id={"fsdp": sibling},
            device_id_type=MESH,
        )

    sibling_kg = pltpu.make_async_remote_copy(
        src_ref=kg,
        dst_ref=kgb.at[pl.ds(tokens, tokens)],
        send_sem=sib_send.at[SIDE * SIDE],
        recv_sem=sib_recv.at[SIDE * SIDE],
        device_id={"fsdp": sibling},
        device_id_type=MESH,
    )

    def far_x(visit):
        def one(e, carry):
            visit(wrap(x + 2) * SIDE + e)
            return carry

        lax.fori_loop(0, SIDE, one, 0)

    def far_y(visit):
        def one(e, carry):
            visit(wrap(x + 3 + e) * SIDE + wrap(y + 2))
            return carry

        lax.fori_loop(0, SIDE - 1, one, 0)

    def rest(visit):
        def one(e, carry):
            visit(wrap(x + 3 + lax.div(e, 3)) * SIDE + wrap(y + 3 + lax.rem(e, 3)))
            return carry

        lax.fori_loop(0, 9, one, 0)

    loads[0].start()
    for visits in (far_x, far_y, rest):
        visits(lambda k: own_block(k).start())
    for copy in loads[1:]:
        copy.start()

    barrier = pltpu.get_barrier_semaphore()
    for peer in (
        sibling,
        device(wrap(x + 1), y),
        device(wrap(x - 1), y),
        device(x, wrap(y + 1)),
        device(x, wrap(y - 1)),
    ):
        pl.semaphore_signal(barrier, inc=1, device_id={"fsdp": peer}, device_id_type=MESH)

    def greet(d, carry):
        pl.semaphore_signal(
            barrier, inc=1, device_id={"island": lax.rem(me + d, islands)}, device_id_type=MESH
        )
        return carry

    lax.fori_loop(1, islands, greet, 0)
    pl.semaphore_wait(barrier, 5 + islands - 1)

    sibling_kg.start()
    for visits in (far_x, far_y, rest):
        visits(lambda k: sibling_block(k).start())

    def neighbour(axis, direction):
        sign = 1 - 2 * direction
        if axis == 0:
            return device(wrap(x + sign), y)
        return device(x, wrap(y + sign))

    def axis_of(phase, half):
        return phase ^ half

    def position(axis):
        return x if axis == 0 else y

    def piece(s, phase, half, group, section):
        if phase == 0:
            return part.at[s, half, pl.ds(group * SIDE + 2 * section, 2)]
        own = position(axis_of(0, half))
        rows = part.shape[3] // 2
        return part.at[s, half, own * SIDE + group, pl.ds(rows * section, rows)]

    def landing(s, phase, half, direction, message):
        buffer = got1 if phase == 0 else got2
        return buffer.at[s, half, direction, message]

    def send(s, phase, half, direction, message):
        axis = axis_of(phase, half)
        pos = position(axis)
        sign = 1 - 2 * direction
        group = wrap(pos + 2) if message == 0 else wrap(pos + sign)
        section = 1 - direction if message == 1 else direction
        return pltpu.make_async_remote_copy(
            src_ref=piece(s, phase, half, group, section),
            dst_ref=landing(s, phase, half, direction, message),
            send_sem=xy_send.at[s, phase, half, direction, message],
            recv_sem=xy_recv.at[s, phase, half, direction, message],
            device_id={"fsdp": neighbour(axis, direction)},
            device_id_type=MESH,
        )

    def first(s, phase, half):
        for direction in (0, 1):
            send(s, phase, half, direction, 0).start()

    def second(s, phase, half):
        for direction in (0, 1):
            send(s, phase, half, direction, 1).start()

    def relay(s, phase, half):
        pos = position(axis_of(phase, half))
        for direction in (0, 1):
            send(s, phase, half, direction, 0).wait_recv()
            target = piece(s, phase, half, wrap(pos + 1 - 2 * direction), direction)
            target[...] += landing(s, phase, half, direction, 0)[...]
            send(s, phase, half, direction, 2).start()

    def arrived(s, phase, half):
        for direction in (0, 1):
            for message in (1, 2):
                send(s, phase, half, direction, message).wait_recv()

    def collect(s, phase, half):
        arrived(s, phase, half)
        pos = position(axis_of(phase, half))
        for section in (0, 1):
            target = piece(s, phase, half, pos, section)
            target[...] += (
                landing(s, phase, half, section, 2)[...]
                + landing(s, phase, half, 1 - section, 1)[...]
            )

    def share_send(s, j):
        owner = STAGES * j + s
        return pltpu.make_async_remote_copy(
            src_ref=step_b.at[s, j],
            dst_ref=zgot.at[me],
            send_sem=zr_send.at[owner],
            recv_sem=zr_recv.at[me],
            device_id={"island": owner},
            device_id_type=MESH,
        )

    def share_from(source):
        return pltpu.make_async_remote_copy(
            src_ref=step_b.at[0, 0],
            dst_ref=zgot.at[source],
            send_sem=zr_send.at[source],
            recv_sem=zr_recv.at[source],
            device_id={"island": source},
            device_id_type=MESH,
        )

    def fresh_send(owner, target):
        return pltpu.make_async_remote_copy(
            src_ref=anb,
            dst_ref=w_out.at[owner],
            send_sem=ag_send.at[target],
            recv_sem=ag_recv.at[owner],
            device_id={"island": target},
            device_id_type=MESH,
        )

    def save_moments(s):
        return (
            pltpu.make_async_copy(mnb.at[:, s], m_out.at[:, s], out_sem.at[0, s]),
            pltpu.make_async_copy(vnb.at[:, s], v_out.at[:, s], out_sem.at[1, s]),
        )

    save_outer = (
        pltpu.make_async_copy(anb, a_out, out_sem.at[2, 0]),
        pltpu.make_async_copy(onb, o_out, out_sem.at[2, 1]),
        pltpu.make_async_copy(anb, w_out.at[me], out_sem.at[2, 2]),
    )

    def inner_step(s):
        for half in (0, 1):
            arrived(s, 1, half)
            pos = position(axis_of(1, half))
            cols = slice(half * half_cols, (half + 1) * half_cols)
            for section in (0, 1):
                js = slice(section * groups // 2, (section + 1) * groups // 2)
                shape = (groups // 2, 8, half_cols)
                grad = (
                    piece(s, 1, half, pos, section)[...]
                    + landing(s, 1, half, section, 2)[...]
                    + landing(s, 1, half, 1 - section, 1)[...]
                ).reshape(shape)
                m_next = beta_first * mb[js, s, :, cols] + (1.0 - beta_first) * grad
                v_next = beta_second * vb[js, s, :, cols] + (1.0 - beta_second) * grad * grad
                old = wb[js, s, :, cols]
                mnb[js, s, :, cols] = m_next
                vnb[js, s, :, cols] = v_next
                step_b[s, js, :, cols] = old - inner_rate * (
                    m_next / (jnp.sqrt(v_next) + epsilon) + decay_rate * old
                )
        for copy in save_moments(s):
            copy.start()

        def one(j, carry):
            @pl.when(STAGES * j + s != me)
            def _():
                share_send(s, j).start()

            return carry

        lax.fori_loop(0, groups, one, 0)

    def outer_step(s):
        @pl.when(lax.rem(me, STAGES) == s)
        def _():
            def add(d, total):
                source = lax.rem(me + d, islands)
                share_from(source).wait_recv()
                return total + zgot[source]

            total = lax.fori_loop(1, islands, add, step_b[s, lax.div(me, STAGES)])
            shift = ab[...] - total / float(islands)
            moment = outer_beta * ob[...] + shift
            anb[...] = ab[...] - outer_rate * (shift + outer_beta * moment)
            onb[...] = moment

            def one(d, carry):
                fresh_send(me, lax.rem(me + d, islands)).start()
                return carry

            lax.fori_loop(1, islands, one, 0)
            for copy in save_outer:
                copy.start()

    def wait_block(k):
        own_block(k).wait()
        sibling_block(k).wait_recv()

    def multiply(half, offset):
        axis = axis_of(0, half)
        group = wrap(position(axis) + offset)

        def one(e, carry):
            k = group * SIDE + e if half == 0 else e * SIDE + group
            product = lax.dot_general(
                actb[k],
                kgb[:, half * half_cols : (half + 1) * half_cols],
                (((0,), (0,)), ((), ())),
                preferred_element_type=jnp.float32,
            )
            for s in range(STAGES):
                for j in range(groups):
                    row = (j * STAGES + s) * 8
                    part[s, half, group * SIDE + e, j * 8 : (j + 1) * 8, :] = product[row : row + 8, :]
            return carry

        lax.fori_loop(0, SIDE, one, 0)

    loads[0].wait()
    sibling_kg.wait_recv()
    far_x(wait_block)
    multiply(0, 2)
    first(0, 0, 0)
    far_y(wait_block)
    multiply(1, 2)
    first(0, 0, 1)
    rest(wait_block)
    for half in (0, 1):
        multiply(half, 1)
        send(0, 0, half, 0, 1).start()
    for half in (0, 1):
        multiply(half, 3)
        send(0, 0, half, 1, 1).start()
    for half in (0, 1):
        multiply(half, 0)
    for copy in loads[1:]:
        copy.wait()

    def stage(t, carry):
        @pl.when(t < STAGES)
        def _():
            for half in (0, 1):
                relay(t, 0, half)

        @pl.when(t + 1 < STAGES)
        def _():
            for half in (0, 1):
                first(t + 1, 0, half)

        @pl.when(t >= 1)
        def _():
            inner_step(t - 1)

        @pl.when(t < STAGES)
        def _():
            for half in (0, 1):
                collect(t, 0, half)
                first(t, 1, half)
                second(t, 1, half)

        @pl.when(t + 1 < STAGES)
        def _():
            for half in (0, 1):
                second(t + 1, 0, half)

        @pl.when(t < STAGES)
        def _():
            for half in (0, 1):
                relay(t, 1, half)

        @pl.when(t >= 1)
        def _():
            outer_step(t - 1)

        return carry

    lax.fori_loop(0, STAGES + 1, stage, 0)

    sibling_kg.wait_send()
    for visits in (far_x, far_y, rest):
        visits(lambda k: sibling_block(k).wait_send())

    def finish(s, carry):
        for phase in (0, 1):
            for half in (0, 1):
                for direction in (0, 1):
                    for message in (0, 1, 2):
                        send(s, phase, half, direction, message).wait_send()
        for copy in save_moments(s):
            copy.wait()
        return carry

    lax.fori_loop(0, STAGES, finish, 0)

    def last(d, carry):
        other = lax.rem(me + d, islands)
        fresh_send(other, me).wait_recv()
        share_from(other).wait_send()
        fresh_send(me, other).wait_send()
        return carry

    lax.fori_loop(1, islands, last, 0)
    for copy in save_outer:
        copy.wait()


def shards(activations, key_grad, island_weight, adam_m, adam_v, anchor, outer_momentum):
    _, tokens, features = activations.shape
    columns = key_grad.shape[2]
    rows = island_weight.shape[1]
    islands = lax.axis_size("island")
    groups = islands // STAGES
    share = rows // islands
    half_cols = columns // 2
    blocks = SIDE * SIDE
    f32 = jnp.float32
    state = (groups, STAGES, share, columns)
    hbm = pl.BlockSpec(memory_space=pl.ANY)
    dma = pltpu.SemaphoreType.DMA
    stage_rows = rows // STAGES

    def kernel(*refs):
        window(islands, *refs)

    m_next, v_next, refreshed, new_anchor, moment = pl.pallas_call(
        kernel,
        out_shape=(
            jax.ShapeDtypeStruct(state, f32),
            jax.ShapeDtypeStruct(state, f32),
            jax.ShapeDtypeStruct((islands, share, columns), f32),
            jax.ShapeDtypeStruct((share, columns), f32),
            jax.ShapeDtypeStruct((share, columns), f32),
        ),
        in_specs=[hbm] * 7,
        out_specs=(hbm,) * 5,
        scratch_shapes=[
            pltpu.VMEM((blocks, 2 * tokens, features // (2 * blocks)), jnp.bfloat16),
            pltpu.VMEM((2 * tokens, columns), jnp.bfloat16),
            pltpu.VMEM((STAGES, 2, blocks, stage_rows, half_cols), f32),
            pltpu.VMEM((STAGES, 2, 2, 3, 2, stage_rows, half_cols), f32),
            pltpu.VMEM((STAGES, 2, 2, 3, stage_rows // 2, half_cols), f32),
            pltpu.VMEM(state, f32),
            pltpu.VMEM(state, f32),
            pltpu.VMEM(state, f32),
            pltpu.VMEM(state, f32),
            pltpu.VMEM(state, f32),
            pltpu.VMEM((STAGES, groups, share, columns), f32),
            pltpu.VMEM((islands, share, columns), f32),
            pltpu.VMEM((share, columns), f32),
            pltpu.VMEM((share, columns), f32),
            pltpu.VMEM((share, columns), f32),
            pltpu.VMEM((share, columns), f32),
            dma((6,)),
            dma((blocks,)),
            dma((blocks + 1,)),
            dma((blocks + 1,)),
            dma((STAGES, 2, 2, 2, 3)),
            dma((STAGES, 2, 2, 2, 3)),
            dma((islands,)),
            dma((islands,)),
            dma((islands,)),
            dma((islands,)),
            dma((3, STAGES)),
        ],
        compiler_params=pltpu.CompilerParams(
            collective_id=0, has_side_effects=True, vmem_limit_bytes=48 * 1024 * 1024
        ),
    )(
        activations[0],
        key_grad[0],
        island_weight.reshape(state),
        adam_m.reshape(state),
        adam_v.reshape(state),
        anchor[0],
        outer_momentum[0],
    )
    return (
        m_next.reshape(island_weight.shape),
        v_next.reshape(island_weight.shape),
        refreshed.reshape(rows, columns),
        new_anchor[None],
        moment[None],
    )


def solution(mesh):
    spec = P("island", "fsdp", None)
    return jax.shard_map(
        shards,
        mesh=mesh,
        in_specs=(spec,) * 7,
        out_specs=(spec, spec, P("fsdp", None), spec, spec),
        check_vma=False,
    )
```

```python
import jax
import jax.numpy as jnp
from jax import lax
from jax.experimental import pallas as pl
from jax.experimental.pallas import tpu as pltpu
from jax.sharding import PartitionSpec as P

beta_first = 0.9
beta_second = 0.95
epsilon = 1e-08
inner_rate = 0.0004
decay_rate = 0.1
outer_beta = 0.9
outer_rate = 0.7

SIDE = 4
STAGES = 4
MESH = pl.DeviceIdType.MESH


def window(
    islands,
    act, kg, weight, adam_m, adam_v, anchor, momentum,
    m_out, v_out, w_out, a_out, o_out,
    actb, kgb, part, got1, got2, wb, mb, vb, mnb, vnb, step_b, zgot, ab, ob, anb, onb,
    load_sem, act_sem, sib_send, sib_recv, xy_send, xy_recv, zr_send, zr_recv, ag_send, ag_recv, out_sem,
):
    me = lax.axis_index("island")
    flat = lax.axis_index("fsdp")
    core = lax.rem(flat, 2)
    chip = lax.div(flat, 2)
    x = lax.div(chip, SIDE)
    y = lax.rem(chip, SIDE)
    tokens = kg.shape[0]
    groups = islands // STAGES
    half_cols = kgb.shape[1] // 2
    sibling = flat + 1 - 2 * core

    def wrap(p):
        return lax.rem(p + 2 * SIDE, SIDE)

    def device(px, py):
        return (px * SIDE + py) * 2 + core

    loads = [
        pltpu.make_async_copy(kg, kgb.at[pl.ds(0, tokens)], load_sem.at[0]),
        pltpu.make_async_copy(weight, wb, load_sem.at[1]),
        pltpu.make_async_copy(adam_m, mb, load_sem.at[2]),
        pltpu.make_async_copy(adam_v, vb, load_sem.at[3]),
        pltpu.make_async_copy(anchor, ab, load_sem.at[4]),
        pltpu.make_async_copy(momentum, ob, load_sem.at[5]),
    ]

    def own_block(k):
        start = pl.multiple_of((2 * k + core) * 128, 128)
        return pltpu.make_async_copy(
            act.at[:, pl.ds(start, 128)], actb.at[k, pl.ds(0, tokens)], act_sem.at[k]
        )

    def sibling_block(k):
        start = pl.multiple_of((2 * k + 1 - core) * 128, 128)
        return pltpu.make_async_remote_copy(
            src_ref=act.at[:, pl.ds(start, 128)],
            dst_ref=actb.at[k, pl.ds(tokens, tokens)],
            send_sem=sib_send.at[k],
            recv_sem=sib_recv.at[k],
            device_id={"fsdp": sibling},
            device_id_type=MESH,
        )

    sibling_kg = pltpu.make_async_remote_copy(
        src_ref=kg,
        dst_ref=kgb.at[pl.ds(tokens, tokens)],
        send_sem=sib_send.at[SIDE * SIDE],
        recv_sem=sib_recv.at[SIDE * SIDE],
        device_id={"fsdp": sibling},
        device_id_type=MESH,
    )

    def far_x(visit):
        def one(e, carry):
            visit(wrap(x + 2) * SIDE + e)
            return carry

        lax.fori_loop(0, SIDE, one, 0)

    def far_y(visit):
        def one(e, carry):
            visit(wrap(x + 3 + e) * SIDE + wrap(y + 2))
            return carry

        lax.fori_loop(0, SIDE - 1, one, 0)

    def rest(visit):
        def one(e, carry):
            visit(wrap(x + 3 + lax.div(e, 3)) * SIDE + wrap(y + 3 + lax.rem(e, 3)))
            return carry

        lax.fori_loop(0, 9, one, 0)

    loads[0].start()
    for visits in (far_x, far_y, rest):
        visits(lambda k: own_block(k).start())
    for copy in loads[1:]:
        copy.start()

    barrier = pltpu.get_barrier_semaphore()
    for peer in (
        sibling,
        device(wrap(x + 1), y),
        device(wrap(x - 1), y),
        device(x, wrap(y + 1)),
        device(x, wrap(y - 1)),
    ):
        pl.semaphore_signal(barrier, inc=1, device_id={"fsdp": peer}, device_id_type=MESH)

    def greet(d, carry):
        pl.semaphore_signal(
            barrier, inc=1, device_id={"island": lax.rem(me + d, islands)}, device_id_type=MESH
        )
        return carry

    lax.fori_loop(1, islands, greet, 0)
    pl.semaphore_wait(barrier, 5 + islands - 1)

    sibling_kg.start()
    for visits in (far_x, far_y, rest):
        visits(lambda k: sibling_block(k).start())

    def neighbour(axis, direction):
        sign = 1 - 2 * direction
        if axis == 0:
            return device(wrap(x + sign), y)
        return device(x, wrap(y + sign))

    def axis_of(phase, half):
        return phase ^ half

    def position(axis):
        return x if axis == 0 else y

    def piece(s, phase, half, group, section):
        if phase == 0:
            return part.at[s, half, pl.ds(group * SIDE + 2 * section, 2)]
        own = position(axis_of(0, half))
        rows = part.shape[3] // 2
        return part.at[s, half, own * SIDE + group, pl.ds(rows * section, rows)]

    def landing(s, phase, half, direction, message):
        buffer = got1 if phase == 0 else got2
        return buffer.at[s, half, direction, message]

    def send(s, phase, half, direction, message):
        axis = axis_of(phase, half)
        pos = position(axis)
        sign = 1 - 2 * direction
        group = wrap(pos + 2) if message == 0 else wrap(pos + sign)
        section = 1 - direction if message == 1 else direction
        return pltpu.make_async_remote_copy(
            src_ref=piece(s, phase, half, group, section),
            dst_ref=landing(s, phase, half, direction, message),
            send_sem=xy_send.at[s, phase, half, direction, message],
            recv_sem=xy_recv.at[s, phase, half, direction, message],
            device_id={"fsdp": neighbour(axis, direction)},
            device_id_type=MESH,
        )

    def first(s, phase, half):
        for direction in (0, 1):
            send(s, phase, half, direction, 0).start()

    def second(s, phase, half):
        for direction in (0, 1):
            send(s, phase, half, direction, 1).start()

    def relay(s, phase, half):
        pos = position(axis_of(phase, half))
        for direction in (0, 1):
            send(s, phase, half, direction, 0).wait_recv()
            target = piece(s, phase, half, wrap(pos + 1 - 2 * direction), direction)
            target[...] += landing(s, phase, half, direction, 0)[...]
            send(s, phase, half, direction, 2).start()

    def arrived(s, phase, half):
        for direction in (0, 1):
            for message in (1, 2):
                send(s, phase, half, direction, message).wait_recv()

    def collect(s, phase, half):
        arrived(s, phase, half)
        pos = position(axis_of(phase, half))
        for section in (0, 1):
            target = piece(s, phase, half, pos, section)
            target[...] += (
                landing(s, phase, half, section, 2)[...]
                + landing(s, phase, half, 1 - section, 1)[...]
            )

    def share_send(s, j):
        owner = STAGES * j + s
        return pltpu.make_async_remote_copy(
            src_ref=step_b.at[s, j],
            dst_ref=zgot.at[me],
            send_sem=zr_send.at[owner],
            recv_sem=zr_recv.at[me],
            device_id={"island": owner},
            device_id_type=MESH,
        )

    def share_from(source):
        return pltpu.make_async_remote_copy(
            src_ref=step_b.at[0, 0],
            dst_ref=zgot.at[source],
            send_sem=zr_send.at[source],
            recv_sem=zr_recv.at[source],
            device_id={"island": source},
            device_id_type=MESH,
        )

    def fresh_send(owner, target):
        return pltpu.make_async_remote_copy(
            src_ref=anb,
            dst_ref=w_out.at[owner],
            send_sem=ag_send.at[target],
            recv_sem=ag_recv.at[owner],
            device_id={"island": target},
            device_id_type=MESH,
        )

    def save_moments(s):
        return (
            pltpu.make_async_copy(mnb.at[:, s], m_out.at[:, s], out_sem.at[0, s]),
            pltpu.make_async_copy(vnb.at[:, s], v_out.at[:, s], out_sem.at[1, s]),
        )

    save_outer = (
        pltpu.make_async_copy(anb, a_out, out_sem.at[2, 0]),
        pltpu.make_async_copy(onb, o_out, out_sem.at[2, 1]),
        pltpu.make_async_copy(anb, w_out.at[me], out_sem.at[2, 2]),
    )

    def inner_step(s):
        for half in (0, 1):
            arrived(s, 1, half)
            pos = position(axis_of(1, half))
            cols = slice(half * half_cols, (half + 1) * half_cols)
            for section in (0, 1):
                js = slice(section * groups // 2, (section + 1) * groups // 2)
                shape = (groups // 2, 8, half_cols)
                grad = (
                    piece(s, 1, half, pos, section)[...]
                    + landing(s, 1, half, section, 2)[...]
                    + landing(s, 1, half, 1 - section, 1)[...]
                ).reshape(shape)
                m_next = beta_first * mb[js, s, :, cols] + (1.0 - beta_first) * grad
                v_next = beta_second * vb[js, s, :, cols] + (1.0 - beta_second) * grad * grad
                old = wb[js, s, :, cols]
                mnb[js, s, :, cols] = m_next
                vnb[js, s, :, cols] = v_next
                step_b[s, js, :, cols] = old - inner_rate * (
                    m_next / (jnp.sqrt(v_next) + epsilon) + decay_rate * old
                )
        for copy in save_moments(s):
            copy.start()

        def one(j, carry):
            @pl.when(STAGES * j + s != me)
            def _():
                share_send(s, j).start()

            return carry

        lax.fori_loop(0, groups, one, 0)

    def outer_step(s):
        @pl.when(lax.rem(me, STAGES) == s)
        def _():
            def add(d, total):
                source = lax.rem(me + d, islands)
                share_from(source).wait_recv()
                return total + zgot[source]

            total = lax.fori_loop(1, islands, add, step_b[s, lax.div(me, STAGES)])
            shift = ab[...] - total / float(islands)
            moment = outer_beta * ob[...] + shift
            anb[...] = ab[...] - outer_rate * (shift + outer_beta * moment)
            onb[...] = moment

            def one(d, carry):
                fresh_send(me, lax.rem(me + d, islands)).start()
                return carry

            lax.fori_loop(1, islands, one, 0)
            for copy in save_outer:
                copy.start()

    def wait_block(k):
        own_block(k).wait()
        sibling_block(k).wait_recv()

    def multiply(half, offset):
        axis = axis_of(0, half)
        group = wrap(position(axis) + offset)

        blocks = [
            actb[group * SIDE + e if half == 0 else e * SIDE + group] for e in range(SIDE)
        ]
        product = lax.dot_general(
            jnp.concatenate(blocks, axis=1),
            kgb[:, half * half_cols : (half + 1) * half_cols],
            (((0,), (0,)), ((), ())),
            preferred_element_type=jnp.float32,
        )
        for e in range(SIDE):
            for s in range(STAGES):
                for j in range(groups):
                    row = e * islands * 8 + (j * STAGES + s) * 8
                    part[s, half, group * SIDE + e, j * 8 : (j + 1) * 8, :] = product[row : row + 8, :]

    loads[0].wait()
    sibling_kg.wait_recv()
    far_x(wait_block)
    multiply(0, 2)
    first(0, 0, 0)
    far_y(wait_block)
    multiply(1, 2)
    first(0, 0, 1)
    rest(wait_block)
    for half in (0, 1):
        multiply(half, 1)
        send(0, 0, half, 0, 1).start()
    for half in (0, 1):
        multiply(half, 3)
        send(0, 0, half, 1, 1).start()
    for half in (0, 1):
        multiply(half, 0)

    def firsts(s):
        for half in (0, 1):
            first(s, 0, half)

    def seconds(s):
        for half in (0, 1):
            second(s, 0, half)

    def relays(s, phase):
        for half in (0, 1):
            relay(s, phase, half)

    def collects(s):
        for half in (0, 1):
            collect(s, 0, half)
            first(s, 1, half)
            second(s, 1, half)

    firsts(1)
    seconds(1)
    relays(0, 0)
    firsts(2)
    relays(1, 0)
    seconds(2)
    collects(0)
    firsts(3)
    relays(2, 0)
    seconds(3)
    collects(1)
    relays(0, 1)
    relays(3, 0)
    for copy in loads[1:]:
        copy.wait()
    inner_step(0)
    collects(2)
    relays(1, 1)
    collects(3)
    relays(2, 1)
    inner_step(1)
    relays(3, 1)
    inner_step(2)
    outer_step(0)
    inner_step(3)
    outer_step(1)
    outer_step(2)
    outer_step(3)

    sibling_kg.wait_send()
    for visits in (far_x, far_y, rest):
        visits(lambda k: sibling_block(k).wait_send())

    def finish(s, carry):
        for phase in (0, 1):
            for half in (0, 1):
                for direction in (0, 1):
                    for message in (0, 1, 2):
                        send(s, phase, half, direction, message).wait_send()
        for copy in save_moments(s):
            copy.wait()
        return carry

    lax.fori_loop(0, STAGES, finish, 0)

    def last(d, carry):
        other = lax.rem(me + d, islands)
        fresh_send(other, me).wait_recv()
        share_from(other).wait_send()
        fresh_send(me, other).wait_send()
        return carry

    lax.fori_loop(1, islands, last, 0)
    for copy in save_outer:
        copy.wait()


def place(*refs):
    sem = refs[-1]
    copies = [pltpu.make_async_copy(refs[i], refs[5 + i], sem.at[i]) for i in range(5)]
    for copy in copies:
        copy.start()
    for copy in copies:
        copy.wait()


def shards(activations, key_grad, island_weight, adam_m, adam_v, anchor, outer_momentum):
    _, tokens, features = activations.shape
    columns = key_grad.shape[2]
    rows = island_weight.shape[1]
    islands = lax.axis_size("island")
    groups = islands // STAGES
    share = rows // islands
    half_cols = columns // 2
    blocks = SIDE * SIDE
    f32 = jnp.float32
    state = (groups, STAGES, share, columns)
    hbm = pl.BlockSpec(memory_space=pl.ANY)
    dma = pltpu.SemaphoreType.DMA
    stage_rows = rows // STAGES

    def kernel(*refs):
        window(islands, *refs)

    results = pl.pallas_call(
        kernel,
        out_shape=(
            jax.ShapeDtypeStruct(state, f32),
            jax.ShapeDtypeStruct(state, f32),
            jax.ShapeDtypeStruct((islands, share, columns), f32),
            jax.ShapeDtypeStruct((share, columns), f32),
            jax.ShapeDtypeStruct((share, columns), f32),
        ),
        in_specs=[hbm] * 7,
        out_specs=(hbm,) * 5,
        scratch_shapes=[
            pltpu.VMEM((blocks, 2 * tokens, features // (2 * blocks)), jnp.bfloat16),
            pltpu.VMEM((2 * tokens, columns), jnp.bfloat16),
            pltpu.VMEM((STAGES, 2, blocks, stage_rows, half_cols), f32),
            pltpu.VMEM((STAGES, 2, 2, 3, 2, stage_rows, half_cols), f32),
            pltpu.VMEM((STAGES, 2, 2, 3, stage_rows // 2, half_cols), f32),
            pltpu.VMEM(state, f32),
            pltpu.VMEM(state, f32),
            pltpu.VMEM(state, f32),
            pltpu.VMEM(state, f32),
            pltpu.VMEM(state, f32),
            pltpu.VMEM((STAGES, groups, share, columns), f32),
            pltpu.VMEM((islands, share, columns), f32),
            pltpu.VMEM((share, columns), f32),
            pltpu.VMEM((share, columns), f32),
            pltpu.VMEM((share, columns), f32),
            pltpu.VMEM((share, columns), f32),
            dma((6,)),
            dma((blocks,)),
            dma((blocks + 1,)),
            dma((blocks + 1,)),
            dma((STAGES, 2, 2, 2, 3)),
            dma((STAGES, 2, 2, 2, 3)),
            dma((islands,)),
            dma((islands,)),
            dma((islands,)),
            dma((islands,)),
            dma((3, STAGES)),
        ],
        compiler_params=pltpu.CompilerParams(
            collective_id=0, has_side_effects=True, vmem_limit_bytes=40 * 1024 * 1024
        ),
    )(
        *(pltpu.with_memory_space_constraint(r, pltpu.MemorySpace.HBM) for r in (activations[0],
        key_grad[0],
        island_weight.reshape(state),
        adam_m.reshape(state),
        adam_v.reshape(state),
        anchor[0],
        outer_momentum[0])),
    )
    m_next, v_next, refreshed, new_anchor, moment = pl.pallas_call(
        place,
        out_shape=tuple(jax.ShapeDtypeStruct(r.shape, f32) for r in results),
        in_specs=[hbm] * 5,
        out_specs=(hbm,) * 5,
        scratch_shapes=[dma((5,))],
        compiler_params=pltpu.CompilerParams(vmem_limit_bytes=1024 * 1024),
    )(*results)
    return (
        m_next.reshape(island_weight.shape),
        v_next.reshape(island_weight.shape),
        refreshed.reshape(rows, columns),
        new_anchor[None],
        moment[None],
    )


def solution(mesh):
    spec = P("island", "fsdp", None)
    return jax.shard_map(
        shards,
        mesh=mesh,
        in_specs=(spec,) * 7,
        out_specs=(spec, spec, P("fsdp", None), spec, spec),
        check_vma=False,
    )
```

```python
import jax
import jax.numpy as jnp
from jax import lax
from jax.experimental import pallas as pl
from jax.experimental.pallas import tpu as pltpu
from jax.sharding import PartitionSpec as P

beta_first = 0.9
beta_second = 0.95
epsilon = 1e-08
inner_rate = 0.0004
decay_rate = 0.1
outer_beta = 0.9
outer_rate = 0.7

SIDE = 4
STAGES = 4
PAIR = 2
MESH = pl.DeviceIdType.MESH


def window(
    islands,
    act, kg, weight, adam_m, adam_v, anchor, momentum,
    m_out, v_out, w_out, a_out, o_out,
    actb, kgb, part, got1, got2, wb, mb, vb, mnb, vnb, step_b, zgot, ab, ob, anb, onb, fresh,
    load_sem, act_sem, sib_send, sib_recv, xy_send, xy_recv, zr_send, zr_recv, ag_send, ag_recv, out_sem,
):
    me = lax.axis_index("island")
    flat = lax.axis_index("fsdp")
    core = lax.rem(flat, 2)
    chip = lax.div(flat, 2)
    x = lax.div(chip, SIDE)
    y = lax.rem(chip, SIDE)
    tokens = kg.shape[0]
    groups = islands // PAIR
    half_cols = kgb.shape[1] // 2
    sibling = flat + 1 - 2 * core

    def wrap(p):
        return lax.rem(p + 2 * SIDE, SIDE)

    def device(px, py):
        return (px * SIDE + py) * 2 + core

    loads = [
        pltpu.make_async_copy(kg, kgb.at[pl.ds(0, tokens)], load_sem.at[0]),
        pltpu.make_async_copy(weight, wb, load_sem.at[1]),
        pltpu.make_async_copy(adam_m, mb, load_sem.at[2]),
        pltpu.make_async_copy(adam_v, vb, load_sem.at[3]),
        pltpu.make_async_copy(anchor, ab, load_sem.at[4]),
        pltpu.make_async_copy(momentum, ob, load_sem.at[5]),
    ]

    def own_block(k):
        start = pl.multiple_of((2 * k + core) * 128, 128)
        return pltpu.make_async_copy(
            act.at[:, pl.ds(start, 128)], actb.at[k, pl.ds(0, tokens)], act_sem.at[k]
        )

    def sibling_block(k):
        start = pl.multiple_of((2 * k + 1 - core) * 128, 128)
        return pltpu.make_async_remote_copy(
            src_ref=act.at[:, pl.ds(start, 128)],
            dst_ref=actb.at[k, pl.ds(tokens, tokens)],
            send_sem=sib_send.at[k],
            recv_sem=sib_recv.at[k],
            device_id={"fsdp": sibling},
            device_id_type=MESH,
        )

    sibling_kg = pltpu.make_async_remote_copy(
        src_ref=kg,
        dst_ref=kgb.at[pl.ds(tokens, tokens)],
        send_sem=sib_send.at[SIDE * SIDE],
        recv_sem=sib_recv.at[SIDE * SIDE],
        device_id={"fsdp": sibling},
        device_id_type=MESH,
    )

    def far_x(visit):
        def one(e, carry):
            visit(wrap(x + 2) * SIDE + e)
            return carry

        lax.fori_loop(0, SIDE, one, 0)

    def far_y(visit):
        def one(e, carry):
            visit(wrap(x + 3 + e) * SIDE + wrap(y + 2))
            return carry

        lax.fori_loop(0, SIDE - 1, one, 0)

    def rest(visit):
        def one(e, carry):
            visit(wrap(x + 3 + lax.div(e, 3)) * SIDE + wrap(y + 3 + lax.rem(e, 3)))
            return carry

        lax.fori_loop(0, 9, one, 0)

    loads[0].start()
    for visits in (far_x, far_y, rest):
        visits(lambda k: own_block(k).start())
    for copy in loads[1:]:
        copy.start()

    barrier = pltpu.get_barrier_semaphore()
    for peer in (
        sibling,
        device(wrap(x + 1), y),
        device(wrap(x - 1), y),
        device(x, wrap(y + 1)),
        device(x, wrap(y - 1)),
    ):
        pl.semaphore_signal(barrier, inc=1, device_id={"fsdp": peer}, device_id_type=MESH)

    def greet(d, carry):
        pl.semaphore_signal(
            barrier, inc=1, device_id={"island": lax.rem(me + d, islands)}, device_id_type=MESH
        )
        return carry

    lax.fori_loop(1, islands, greet, 0)
    pl.semaphore_wait(barrier, 5 + islands - 1)

    sibling_kg.start()
    for visits in (far_x, far_y, rest):
        visits(lambda k: sibling_block(k).start())

    def neighbour(axis, direction):
        sign = 1 - 2 * direction
        if axis == 0:
            return device(wrap(x + sign), y)
        return device(x, wrap(y + sign))

    def axis_of(phase, half):
        return phase ^ half

    def position(axis):
        return x if axis == 0 else y

    def piece(s, phase, half, group, section):
        if phase == 0:
            return part.at[s, half, pl.ds(group * SIDE + 2 * section, 2)]
        own = position(axis_of(0, half))
        rows = part.shape[3] // 2
        return part.at[s, half, own * SIDE + group, pl.ds(rows * section, rows)]

    def landing(s, phase, half, direction, message):
        buffer = got1 if phase == 0 else got2
        return buffer.at[s, half, direction, message]

    def send(s, phase, half, direction, message):
        axis = axis_of(phase, half)
        pos = position(axis)
        sign = 1 - 2 * direction
        group = wrap(pos + 2) if message == 0 else wrap(pos + sign)
        section = 1 - direction if message == 1 else direction
        return pltpu.make_async_remote_copy(
            src_ref=piece(s, phase, half, group, section),
            dst_ref=landing(s, phase, half, direction, message),
            send_sem=xy_send.at[s, phase, half, direction, message],
            recv_sem=xy_recv.at[s, phase, half, direction, message],
            device_id={"fsdp": neighbour(axis, direction)},
            device_id_type=MESH,
        )

    def first(s, phase, half):
        for direction in (0, 1):
            send(s, phase, half, direction, 0).start()

    def second(s, phase, half):
        for direction in (0, 1):
            send(s, phase, half, direction, 1).start()

    def relay(s, phase, half):
        pos = position(axis_of(phase, half))
        for direction in (0, 1):
            send(s, phase, half, direction, 0).wait_recv()
            target = piece(s, phase, half, wrap(pos + 1 - 2 * direction), direction)
            target[...] += landing(s, phase, half, direction, 0)[...]
            send(s, phase, half, direction, 2).start()

    def arrived(s, phase, half):
        for direction in (0, 1):
            for message in (1, 2):
                send(s, phase, half, direction, message).wait_recv()

    def collect(s, phase, half):
        arrived(s, phase, half)
        pos = position(axis_of(phase, half))
        for section in (0, 1):
            target = piece(s, phase, half, pos, section)
            target[...] += (
                landing(s, phase, half, section, 2)[...]
                + landing(s, phase, half, 1 - section, 1)[...]
            )

    def share_send(s, j):
        chunk, parity = s // PAIR, s % PAIR
        owner = PAIR * j + parity
        return pltpu.make_async_remote_copy(
            src_ref=step_b.at[s, j],
            dst_ref=zgot.at[chunk, me],
            send_sem=zr_send.at[chunk, owner],
            recv_sem=zr_recv.at[chunk, me],
            device_id={"island": owner},
            device_id_type=MESH,
        )

    def share_from(chunk, source):
        return pltpu.make_async_remote_copy(
            src_ref=step_b.at[0, 0],
            dst_ref=zgot.at[chunk, source],
            send_sem=zr_send.at[chunk, source],
            recv_sem=zr_recv.at[chunk, source],
            device_id={"island": source},
            device_id_type=MESH,
        )

    def fresh_send(chunk, owner, target):
        return pltpu.make_async_remote_copy(
            src_ref=fresh.at[chunk],
            dst_ref=w_out.at[chunk, owner],
            send_sem=ag_send.at[chunk, target],
            recv_sem=ag_recv.at[chunk, owner],
            device_id={"island": target},
            device_id_type=MESH,
        )

    save_moments = (
        pltpu.make_async_copy(mnb, m_out, out_sem.at[0]),
        pltpu.make_async_copy(vnb, v_out, out_sem.at[1]),
    )
    save_outer = (
        pltpu.make_async_copy(anb, a_out, out_sem.at[2]),
        pltpu.make_async_copy(onb, o_out, out_sem.at[3]),
        pltpu.make_async_copy(fresh, w_out.at[:, me], out_sem.at[4]),
    )

    def columns(chunk, half):
        return slice(half * half_cols + chunk * 128, half * half_cols + (chunk + 1) * 128)

    def inner_step(s):
        chunk, parity = s // PAIR, s % PAIR
        for half in (0, 1):
            arrived(s, 1, half)
            pos = position(axis_of(1, half))
            cols = columns(chunk, half)
            for section in (0, 1):
                js = slice(section * groups // 2, (section + 1) * groups // 2)
                grad = (
                    piece(s, 1, half, pos, section)[...]
                    + landing(s, 1, half, section, 2)[...]
                    + landing(s, 1, half, 1 - section, 1)[...]
                ).reshape(groups // 2, 8, 128)
                m_next = beta_first * mb[js, parity, :, cols] + (1.0 - beta_first) * grad
                v_next = beta_second * vb[js, parity, :, cols] + (1.0 - beta_second) * grad * grad
                old = wb[js, parity, :, cols]
                mnb[js, parity, :, cols] = m_next
                vnb[js, parity, :, cols] = v_next
                step_b[s, js, half] = old - inner_rate * (
                    m_next / (jnp.sqrt(v_next) + epsilon) + decay_rate * old
                )

        def one(j, carry):
            @pl.when(PAIR * j + parity != me)
            def _():
                share_send(s, j).start()

            return carry

        lax.fori_loop(0, groups, one, 0)

    def outer_step(s):
        chunk, parity = s // PAIR, s % PAIR

        @pl.when(lax.rem(me, PAIR) == parity)
        def _():
            def add(d, total):
                source = lax.rem(me + d, islands)
                share_from(chunk, source).wait_recv()
                return total + zgot[chunk, source]

            total = lax.fori_loop(1, islands, add, step_b[s, lax.div(me, PAIR)])
            for half in (0, 1):
                cols = columns(chunk, half)
                old = ab[:, cols]
                shift = old - total[half] / float(islands)
                moment = outer_beta * ob[:, cols] + shift
                new = old - outer_rate * (shift + outer_beta * moment)
                fresh[chunk, half] = new
                anb[:, cols] = new
                onb[:, cols] = moment

            def one(d, carry):
                fresh_send(chunk, me, lax.rem(me + d, islands)).start()
                return carry

            lax.fori_loop(1, islands, one, 0)

    def wait_block(k):
        own_block(k).wait()
        sibling_block(k).wait_recv()

    def multiply(half, offset):
        axis = axis_of(0, half)
        group = wrap(position(axis) + offset)

        blocks = [
            actb[group * SIDE + e if half == 0 else e * SIDE + group] for e in range(SIDE)
        ]
        product = lax.dot_general(
            jnp.concatenate(blocks, axis=1),
            kgb[:, half * half_cols : (half + 1) * half_cols],
            (((0,), (0,)), ((), ())),
            preferred_element_type=jnp.float32,
        )
        for e in range(SIDE):
            for s in range(STAGES):
                chunk, parity = s // PAIR, s % PAIR
                for j in range(groups):
                    row = (e * islands + PAIR * j + parity) * 8
                    part[s, half, group * SIDE + e, j * 8 : (j + 1) * 8, :] = product[
                        row : row + 8, chunk * 128 : (chunk + 1) * 128
                    ]

    loads[0].wait()
    sibling_kg.wait_recv()
    far_x(wait_block)
    multiply(0, 2)
    first(0, 0, 0)
    far_y(wait_block)
    multiply(1, 2)
    first(0, 0, 1)
    rest(wait_block)
    for half in (0, 1):
        multiply(half, 1)
        send(0, 0, half, 0, 1).start()
    for half in (0, 1):
        multiply(half, 3)
        send(0, 0, half, 1, 1).start()
    for half in (0, 1):
        multiply(half, 0)

    def firsts(s):
        for half in (0, 1):
            first(s, 0, half)

    def seconds(s):
        for half in (0, 1):
            second(s, 0, half)

    def relays(s, phase):
        for half in (0, 1):
            relay(s, phase, half)

    def collects(s):
        for half in (0, 1):
            collect(s, 0, half)
            first(s, 1, half)
            second(s, 1, half)

    firsts(1)
    seconds(1)
    relays(0, 0)
    firsts(2)
    relays(1, 0)
    seconds(2)
    collects(0)
    firsts(3)
    relays(2, 0)
    collects(1)
    relays(0, 1)
    seconds(3)
    relays(3, 0)
    collects(2)
    relays(1, 1)
    for copy in loads[1:]:
        copy.wait()
    inner_step(0)
    collects(3)
    relays(2, 1)
    inner_step(1)
    relays(3, 1)
    inner_step(2)
    inner_step(3)
    for copy in save_moments:
        copy.start()
    for s in range(STAGES):
        outer_step(s)
    for copy in save_outer:
        copy.start()

    sibling_kg.wait_send()
    for visits in (far_x, far_y, rest):
        visits(lambda k: sibling_block(k).wait_send())

    def finish(s, carry):
        for phase in (0, 1):
            for half in (0, 1):
                for direction in (0, 1):
                    for message in (0, 1, 2):
                        send(s, phase, half, direction, message).wait_send()
        return carry

    lax.fori_loop(0, STAGES, finish, 0)

    def last(d, carry):
        other = lax.rem(me + d, islands)
        for chunk in (0, 1):
            fresh_send(chunk, other, me).wait_recv()
            share_from(chunk, other).wait_send()
            fresh_send(chunk, me, other).wait_send()
        return carry

    lax.fori_loop(1, islands, last, 0)
    for copy in save_moments + save_outer:
        copy.wait()


def place(m, v, w, a, o, m_out, v_out, w_out, a_out, o_out, sem):
    pairs = [(m, m_out), (v, v_out), (a, a_out), (o, o_out)]
    for half in (0, 1):
        for chunk in (0, 1):
            start = (2 * half + chunk) * 128
            pairs.append((w.at[chunk, :, half], w_out.at[:, :, start : start + 128]))
    copies = [pltpu.make_async_copy(old, new, sem.at[i]) for i, (old, new) in enumerate(pairs)]
    for copy in copies:
        copy.start()
    for copy in copies:
        copy.wait()


def shards(activations, key_grad, island_weight, adam_m, adam_v, anchor, outer_momentum):
    _, tokens, features = activations.shape
    columns = key_grad.shape[2]
    rows = island_weight.shape[1]
    islands = lax.axis_size("island")
    groups = islands // PAIR
    share = rows // islands
    blocks = SIDE * SIDE
    f32 = jnp.float32
    state = (groups, PAIR, share, columns)
    hbm = pl.BlockSpec(memory_space=pl.ANY)
    dma = pltpu.SemaphoreType.DMA
    stage_rows = rows // PAIR
    tiles = (2, share, 128)

    def kernel(*refs):
        window(islands, *refs)

    results = pl.pallas_call(
        kernel,
        out_shape=(
            jax.ShapeDtypeStruct(state, f32),
            jax.ShapeDtypeStruct(state, f32),
            jax.ShapeDtypeStruct((2, islands) + tiles, f32),
            jax.ShapeDtypeStruct((share, columns), f32),
            jax.ShapeDtypeStruct((share, columns), f32),
        ),
        in_specs=[hbm] * 7,
        out_specs=(hbm,) * 5,
        scratch_shapes=[
            pltpu.VMEM((blocks, 2 * tokens, features // (2 * blocks)), jnp.bfloat16),
            pltpu.VMEM((2 * tokens, columns), jnp.bfloat16),
            pltpu.VMEM((STAGES, 2, blocks, stage_rows, 128), f32),
            pltpu.VMEM((STAGES, 2, 2, 3, 2, stage_rows, 128), f32),
            pltpu.VMEM((STAGES, 2, 2, 3, stage_rows // 2, 128), f32),
            pltpu.VMEM(state, f32),
            pltpu.VMEM(state, f32),
            pltpu.VMEM(state, f32),
            pltpu.VMEM(state, f32),
            pltpu.VMEM(state, f32),
            pltpu.VMEM((STAGES, groups) + tiles, f32),
            pltpu.VMEM((2, islands) + tiles, f32),
            pltpu.VMEM((share, columns), f32),
            pltpu.VMEM((share, columns), f32),
            pltpu.VMEM((share, columns), f32),
            pltpu.VMEM((share, columns), f32),
            pltpu.VMEM((2,) + tiles, f32),
            dma((6,)),
            dma((blocks,)),
            dma((blocks + 1,)),
            dma((blocks + 1,)),
            dma((STAGES, 2, 2, 2, 3)),
            dma((STAGES, 2, 2, 2, 3)),
            dma((2, islands)),
            dma((2, islands)),
            dma((2, islands)),
            dma((2, islands)),
            dma((5,)),
        ],
        compiler_params=pltpu.CompilerParams(
            collective_id=0, has_side_effects=True, vmem_limit_bytes=40 * 1024 * 1024
        ),
    )(
        *(pltpu.with_memory_space_constraint(r, pltpu.MemorySpace.HBM) for r in (activations[0],
        key_grad[0],
        island_weight.reshape(state),
        adam_m.reshape(state),
        adam_v.reshape(state),
        anchor[0],
        outer_momentum[0])),
    )
    m_next, v_next, refreshed, new_anchor, moment = pl.pallas_call(
        place,
        out_shape=tuple(
            jax.ShapeDtypeStruct(shape, f32)
            for shape in (state, state, (islands, share, columns), (share, columns), (share, columns))
        ),
        in_specs=[hbm] * 5,
        out_specs=(hbm,) * 5,
        scratch_shapes=[dma((8,))],
        compiler_params=pltpu.CompilerParams(vmem_limit_bytes=1024 * 1024),
    )(*results)
    return (
        m_next.reshape(island_weight.shape),
        v_next.reshape(island_weight.shape),
        refreshed.reshape(rows, columns),
        new_anchor[None],
        moment[None],
    )


def solution(mesh):
    spec = P("island", "fsdp", None)
    return jax.shard_map(
        shards,
        mesh=mesh,
        in_specs=(spec,) * 7,
        out_specs=(spec, spec, P("fsdp", None), spec, spec),
        check_vma=False,
    )
```

```python
import jax
import jax.numpy as jnp
from jax import lax
from jax.experimental import pallas as pl
from jax.experimental.pallas import tpu as pltpu
from jax.sharding import PartitionSpec as P

beta_first = 0.9
beta_second = 0.95
epsilon = 1e-08
inner_rate = 0.0004
decay_rate = 0.1
outer_beta = 0.9
outer_rate = 0.7

SIDE = 4
PAIR = 2
STAGES = 2 * PAIR
MESH = pl.DeviceIdType.MESH


def window(
    islands,
    act, kg, weight, adam_m, adam_v, anchor, momentum,
    m_out, v_out, w_out, a_out, o_out,
    actb, kgb, part, got1, got2, wb, mb, vb, mnb, vnb, step_b, zgot, ab, ob, anb, onb, fresh,
    load_sem, act_sem, sib_send, sib_recv, xy_send, xy_relay, xy_last, zr_send, zr_recv, ag_send, ag_recv, out_sem,
):
    me = lax.axis_index("island")
    flat = lax.axis_index("fsdp")
    core = lax.rem(flat, 2)
    chip = lax.div(flat, 2)
    x = lax.div(chip, SIDE)
    y = lax.rem(chip, SIDE)
    tokens = kg.shape[0]
    groups = islands // PAIR
    half_cols = kgb.shape[1] // 2
    sibling = flat + 1 - 2 * core

    def wrap(p):
        return lax.rem(p + 2 * SIDE, SIDE)

    def device(px, py):
        return (px * SIDE + py) * 2 + core

    loads = [
        pltpu.make_async_copy(kg, kgb.at[pl.ds(0, tokens)], load_sem.at[0]),
        pltpu.make_async_copy(weight, wb, load_sem.at[1]),
        pltpu.make_async_copy(adam_m, mb, load_sem.at[2]),
        pltpu.make_async_copy(adam_v, vb, load_sem.at[3]),
        pltpu.make_async_copy(anchor, ab, load_sem.at[4]),
        pltpu.make_async_copy(momentum, ob, load_sem.at[5]),
    ]

    def own_block(k):
        start = pl.multiple_of((2 * k + core) * 128, 128)
        return pltpu.make_async_copy(
            act.at[:, pl.ds(start, 128)], actb.at[k, pl.ds(0, tokens)], act_sem.at[k]
        )

    def sibling_block(k):
        start = pl.multiple_of((2 * k + 1 - core) * 128, 128)
        return pltpu.make_async_remote_copy(
            src_ref=act.at[:, pl.ds(start, 128)],
            dst_ref=actb.at[k, pl.ds(tokens, tokens)],
            send_sem=sib_send.at[k],
            recv_sem=sib_recv.at[k],
            device_id={"fsdp": sibling},
            device_id_type=MESH,
        )

    def sibling_kg(half):
        cols = slice(half * half_cols, (half + 1) * half_cols)
        return pltpu.make_async_remote_copy(
            src_ref=kg.at[:, cols],
            dst_ref=kgb.at[pl.ds(tokens, tokens), cols],
            send_sem=sib_send.at[SIDE * SIDE + half],
            recv_sem=sib_recv.at[SIDE * SIDE + half],
            device_id={"fsdp": sibling},
            device_id_type=MESH,
        )

    def far_x(visit):
        def one(e, carry):
            visit(wrap(x + 2) * SIDE + e)
            return carry

        lax.fori_loop(0, SIDE, one, 0)

    def far_y(visit):
        def one(e, carry):
            visit(wrap(x + 3 + e) * SIDE + wrap(y + 2))
            return carry

        lax.fori_loop(0, SIDE - 1, one, 0)

    def rest(visit):
        def one(e, carry):
            visit(wrap(x + 3 + lax.div(e, 3)) * SIDE + wrap(y + 3 + lax.rem(e, 3)))
            return carry

        lax.fori_loop(0, 9, one, 0)

    barrier = pltpu.get_barrier_semaphore()
    for peer in (
        sibling,
        device(wrap(x + 1), y),
        device(wrap(x - 1), y),
        device(x, wrap(y + 1)),
        device(x, wrap(y - 1)),
    ):
        pl.semaphore_signal(barrier, inc=1, device_id={"fsdp": peer}, device_id_type=MESH)

    def greet(d, carry):
        pl.semaphore_signal(
            barrier, inc=1, device_id={"island": lax.rem(me + d, islands)}, device_id_type=MESH
        )
        return carry

    lax.fori_loop(1, islands, greet, 0)
    pl.semaphore_wait(barrier, 5 + islands - 1)

    def both(k):
        sibling_block(k).start()
        own_block(k).start()

    sibling_kg(0).start()
    loads[0].start()
    far_x(both)
    sibling_kg(1).start()
    far_y(both)
    rest(both)
    for copy in loads[1:]:
        copy.start()

    def neighbour(axis, direction):
        sign = 1 - 2 * direction
        if axis == 0:
            return device(wrap(x + sign), y)
        return device(x, wrap(y + sign))

    def axis_of(phase, half):
        return phase ^ half

    def position(axis):
        return x if axis == 0 else y

    def piece(s, phase, half, group, section):
        if phase == 0:
            return part.at[s, half, pl.ds(group * SIDE + 2 * section, 2)]
        own = position(axis_of(0, half))
        rows = part.shape[3] // 2
        return part.at[s, half, own * SIDE + group, pl.ds(rows * section, rows)]

    def landing(s, phase, half, direction, message):
        buffer = got1 if phase == 0 else got2
        return buffer.at[s, half, direction, message]

    def send(s, phase, half, direction, message):
        axis = axis_of(phase, half)
        pos = position(axis)
        sign = 1 - 2 * direction
        group = wrap(pos + 2) if message == 0 else wrap(pos + sign)
        section = 1 - direction if message == 1 else direction
        return pltpu.make_async_remote_copy(
            src_ref=piece(s, phase, half, group, section),
            dst_ref=landing(s, phase, half, direction, message),
            send_sem=xy_send.at[s, phase],
            recv_sem=(
                xy_relay.at[s, phase, half, direction] if message == 0 else xy_last.at[s, phase, half]
            ),
            device_id={"fsdp": neighbour(axis, direction)},
            device_id_type=MESH,
        )

    def first(s, phase, half):
        for direction in (0, 1):
            send(s, phase, half, direction, 0).start()

    def second(s, phase, half):
        for direction in (0, 1):
            send(s, phase, half, direction, 1).start()

    def relay(s, phase, half):
        pos = position(axis_of(phase, half))
        for direction in (0, 1):
            send(s, phase, half, direction, 0).wait_recv()
            target = piece(s, phase, half, wrap(pos + 1 - 2 * direction), direction)
            target[...] += landing(s, phase, half, direction, 0)[...]
            send(s, phase, half, direction, 2).start()

    def arrived(s, phase, half):
        buffer = got1 if phase == 0 else got2
        landed = buffer.at[s, half, :, pl.ds(1, 2)]
        pltpu.make_async_copy(landed, landed, xy_last.at[s, phase, half]).wait()

    def collect(s, phase, half):
        arrived(s, phase, half)
        pos = position(axis_of(phase, half))
        for section in (0, 1):
            target = piece(s, phase, half, pos, section)
            target[...] += (
                landing(s, phase, half, section, 2)[...]
                + landing(s, phase, half, 1 - section, 1)[...]
            )

    def share_send(s, j):
        chunk, parity = s // PAIR, s % PAIR
        owner = PAIR * j + parity
        return pltpu.make_async_remote_copy(
            src_ref=step_b.at[s, j],
            dst_ref=zgot.at[chunk, me],
            send_sem=zr_send.at[chunk],
            recv_sem=zr_recv.at[chunk],
            device_id={"island": owner},
            device_id_type=MESH,
        )

    def all_of(chunk, sem):
        others = zgot.at[chunk, pl.ds(0, islands - 1)]
        return pltpu.make_async_copy(others, others, sem.at[chunk])

    def fresh_send(chunk, owner, target):
        return pltpu.make_async_remote_copy(
            src_ref=fresh.at[chunk],
            dst_ref=w_out.at[chunk, owner],
            send_sem=ag_send.at[chunk],
            recv_sem=ag_recv.at[chunk],
            device_id={"island": target},
            device_id_type=MESH,
        )

    save_moments = (
        pltpu.make_async_copy(mnb, m_out, out_sem.at[0]),
        pltpu.make_async_copy(vnb, v_out, out_sem.at[1]),
    )
    save_outer = (
        pltpu.make_async_copy(anb, a_out, out_sem.at[2]),
        pltpu.make_async_copy(onb, o_out, out_sem.at[3]),
        pltpu.make_async_copy(fresh, w_out.at[:, me], out_sem.at[4]),
    )

    def columns(chunk, half):
        return slice(half * half_cols + chunk * 128, half * half_cols + (chunk + 1) * 128)

    def inner_step(s):
        chunk, parity = s // PAIR, s % PAIR
        for half in (0, 1):
            arrived(s, 1, half)
            pos = position(axis_of(1, half))
            cols = columns(chunk, half)
            for section in (0, 1):
                js = slice(section * groups // 2, (section + 1) * groups // 2)
                grad = (
                    piece(s, 1, half, pos, section)[...]
                    + landing(s, 1, half, section, 2)[...]
                    + landing(s, 1, half, 1 - section, 1)[...]
                ).reshape(groups // 2, 8, 128)
                m_next = beta_first * mb[js, parity, :, cols] + (1.0 - beta_first) * grad
                v_next = beta_second * vb[js, parity, :, cols] + (1.0 - beta_second) * grad * grad
                old = wb[js, parity, :, cols]
                mnb[js, parity, :, cols] = m_next
                vnb[js, parity, :, cols] = v_next
                step_b[s, js, half] = old - inner_rate * (
                    m_next / (jnp.sqrt(v_next) + epsilon) + decay_rate * old
                )

        def one(j, carry):
            @pl.when(PAIR * j + parity != me)
            def _():
                share_send(s, j).start()

            return carry

        lax.fori_loop(0, groups, one, 0)

    def outer_step(s):
        chunk, parity = s // PAIR, s % PAIR

        @pl.when(lax.rem(me, PAIR) == parity)
        def _():
            zgot[chunk, me] = step_b[s, lax.div(me, PAIR)]
            all_of(chunk, zr_recv).wait()
            total = jnp.sum(zgot[chunk], axis=0)
            for half in (0, 1):
                cols = columns(chunk, half)
                old = ab[:, cols]
                shift = old - total[half] / float(islands)
                moment = outer_beta * ob[:, cols] + shift
                new = old - outer_rate * (shift + outer_beta * moment)
                fresh[chunk, half] = new
                anb[:, cols] = new
                onb[:, cols] = moment

            def one(d, carry):
                fresh_send(chunk, me, lax.rem(me + d, islands)).start()
                return carry

            lax.fori_loop(1, islands, one, 0)

    def wait_block(k):
        own_block(k).wait()
        sibling_block(k).wait_recv()

    def multiply(half, offset):
        axis = axis_of(0, half)
        group = wrap(position(axis) + offset)

        blocks = [
            actb[group * SIDE + e if half == 0 else e * SIDE + group] for e in range(SIDE)
        ]
        product = lax.dot_general(
            jnp.concatenate(blocks, axis=1),
            kgb[:, half * half_cols : (half + 1) * half_cols],
            (((0,), (0,)), ((), ())),
            preferred_element_type=jnp.float32,
        )
        for e in range(SIDE):
            for s in range(STAGES):
                chunk, parity = s // PAIR, s % PAIR
                for j in range(groups):
                    row = (e * islands + PAIR * j + parity) * 8
                    part[s, half, group * SIDE + e, j * 8 : (j + 1) * 8, :] = product[
                        row : row + 8, chunk * 128 : (chunk + 1) * 128
                    ]

    early_first = (0, 1)
    early_second = (0, 1)
    loads[0].wait()
    sibling_kg(0).wait_recv()
    far_x(wait_block)
    multiply(0, 2)
    for s in early_first:
        first(s, 0, 0)
    sibling_kg(1).wait_recv()
    far_y(wait_block)
    multiply(1, 2)
    for s in early_first:
        first(s, 0, 1)
    rest(wait_block)
    for direction, offset in ((0, 1), (1, 3)):
        for half in (0, 1):
            multiply(half, offset)
            for s in early_second:
                send(s, 0, half, direction, 1).start()
    for half in (0, 1):
        multiply(half, 0)

    def firsts(s):
        for half in (0, 1):
            first(s, 0, half)

    def seconds(s):
        for half in (0, 1):
            second(s, 0, half)

    def relays_far(s):
        for half in (0, 1):
            relay(s, 0, half)

    def relays_near(s):
        for half in (0, 1):
            relay(s, 1, half)

    def collects(s):
        for half in (0, 1):
            collect(s, 0, half)
            first(s, 1, half)
            second(s, 1, half)

    relays_far(0)
    firsts(2)
    relays_far(1)
    seconds(2)
    collects(0)
    firsts(3)
    relays_far(2)
    collects(1)
    relays_near(0)
    seconds(3)
    relays_far(3)
    collects(2)
    relays_near(1)
    for copy in loads[1:]:
        copy.wait()
    inner_step(0)
    collects(3)
    relays_near(2)
    inner_step(1)
    relays_near(3)
    inner_step(2)
    inner_step(3)
    for copy in save_moments:
        copy.start()
    outer_step(0)
    outer_step(1)
    outer_step(2)
    outer_step(3)
    for copy in save_outer:
        copy.start()

    for half in (0, 1):
        sibling_kg(half).wait_send()
    for visits in (far_x, far_y, rest):
        visits(lambda k: sibling_block(k).wait_send())

    for s in range(STAGES):
        for phase, buffer in ((0, got1), (1, got2)):
            pltpu.make_async_copy(buffer.at[s], buffer.at[s], xy_send.at[s, phase]).wait()
    for chunk in (0, 1):
        all_of(chunk, zr_send).wait()
        all_of(chunk, ag_recv).wait()
    for chunk in (0, 1):
        all_of(chunk, ag_send).wait()
    for copy in save_moments + save_outer:
        copy.wait()


def place(m, v, w, a, o, m_out, v_out, w_out, a_out, o_out, sem):
    pairs = [(m, m_out), (v, v_out), (a, a_out), (o, o_out)]
    for half in (0, 1):
        for chunk in (0, 1):
            start = (2 * half + chunk) * 128
            pairs.append((w.at[chunk, :, half], w_out.at[:, :, start : start + 128]))
    copies = [pltpu.make_async_copy(old, new, sem.at[i]) for i, (old, new) in enumerate(pairs)]
    for copy in copies:
        copy.start()
    for copy in copies:
        copy.wait()


def shards(activations, key_grad, island_weight, adam_m, adam_v, anchor, outer_momentum):
    _, tokens, features = activations.shape
    columns = key_grad.shape[2]
    rows = island_weight.shape[1]
    islands = lax.axis_size("island")
    groups = islands // PAIR
    share = rows // islands
    blocks = SIDE * SIDE
    f32 = jnp.float32
    state = (groups, PAIR, share, columns)
    hbm = pl.BlockSpec(memory_space=pl.ANY)
    dma = pltpu.SemaphoreType.DMA
    stage_rows = rows // PAIR
    tiles = (2, share, 128)

    def kernel(*refs):
        window(islands, *refs)

    results = pl.pallas_call(
        kernel,
        out_shape=(
            jax.ShapeDtypeStruct(state, f32),
            jax.ShapeDtypeStruct(state, f32),
            jax.ShapeDtypeStruct((2, islands) + tiles, f32),
            jax.ShapeDtypeStruct((share, columns), f32),
            jax.ShapeDtypeStruct((share, columns), f32),
        ),
        in_specs=[hbm] * 7,
        out_specs=(hbm,) * 5,
        scratch_shapes=[
            pltpu.VMEM((blocks, 2 * tokens, features // (2 * blocks)), jnp.bfloat16),
            pltpu.VMEM((2 * tokens, columns), jnp.bfloat16),
            pltpu.VMEM((STAGES, 2, blocks, stage_rows, 128), f32),
            pltpu.VMEM((STAGES, 2, 2, 3, 2, stage_rows, 128), f32),
            pltpu.VMEM((STAGES, 2, 2, 3, stage_rows // 2, 128), f32),
            pltpu.VMEM(state, f32),
            pltpu.VMEM(state, f32),
            pltpu.VMEM(state, f32),
            pltpu.VMEM(state, f32),
            pltpu.VMEM(state, f32),
            pltpu.VMEM((STAGES, groups) + tiles, f32),
            pltpu.VMEM((2, islands) + tiles, f32),
            pltpu.VMEM((share, columns), f32),
            pltpu.VMEM((share, columns), f32),
            pltpu.VMEM((share, columns), f32),
            pltpu.VMEM((share, columns), f32),
            pltpu.VMEM((2,) + tiles, f32),
            dma((6,)),
            dma((blocks,)),
            dma((blocks + 2,)),
            dma((blocks + 2,)),
            dma((STAGES, 2)),
            dma((STAGES, 2, 2, 2)),
            dma((STAGES, 2, 2)),
            dma((2,)),
            dma((2,)),
            dma((2,)),
            dma((2,)),
            dma((5,)),
        ],
        compiler_params=pltpu.CompilerParams(
            collective_id=0, has_side_effects=True, vmem_limit_bytes=40 * 1024 * 1024
        ),
    )(
        *(pltpu.with_memory_space_constraint(r, pltpu.MemorySpace.HBM) for r in (activations[0],
        key_grad[0],
        island_weight.reshape(state),
        adam_m.reshape(state),
        adam_v.reshape(state),
        anchor[0],
        outer_momentum[0])),
    )
    m_next, v_next, refreshed, new_anchor, moment = pl.pallas_call(
        place,
        out_shape=tuple(
            jax.ShapeDtypeStruct(shape, f32)
            for shape in (state, state, (islands, share, columns), (share, columns), (share, columns))
        ),
        in_specs=[hbm] * 5,
        out_specs=(hbm,) * 5,
        scratch_shapes=[dma((8,))],
        compiler_params=pltpu.CompilerParams(vmem_limit_bytes=1024 * 1024),
    )(*results)
    return (
        m_next.reshape(island_weight.shape),
        v_next.reshape(island_weight.shape),
        refreshed.reshape(rows, columns),
        new_anchor[None],
        moment[None],
    )


def solution(mesh):
    spec = P("island", "fsdp", None)
    return jax.shard_map(
        shards,
        mesh=mesh,
        in_specs=(spec,) * 7,
        out_specs=(spec, spec, P("fsdp", None), spec, spec),
        check_vma=False,
    )
```

```python
import jax
import jax.numpy as jnp
from jax import lax
from jax.experimental import pallas as pl
from jax.experimental.pallas import tpu as pltpu
from jax.sharding import PartitionSpec as P

beta_first = 0.9
beta_second = 0.95
epsilon = 1e-08
inner_rate = 0.0004
decay_rate = 0.1
outer_beta = 0.9
outer_rate = 0.7

SIDE = 4
PAIR = 2
STAGES = 2 * PAIR
MESH = pl.DeviceIdType.MESH


def window(
    islands,
    act, kg, weight, adam_m, adam_v, anchor, momentum,
    m_out, v_out, w_out, a_out, o_out,
    actb, kgb, part, got1, got2, wb, mb, vb, mnb, vnb, step_b, zgot, ab, ob, anb, onb, fresh,
    load_sem, act_sem, sib_send, sib_recv, xy_send, xy_relay, xy_last, zr_send, zr_recv, ag_send, ag_recv, out_sem,
):
    me = lax.axis_index("island")
    flat = lax.axis_index("fsdp")
    core = lax.rem(flat, 2)
    chip = lax.div(flat, 2)
    x = lax.div(chip, SIDE)
    y = lax.rem(chip, SIDE)
    tokens = kg.shape[0]
    groups = islands // PAIR
    half_cols = kgb.shape[1] // 2
    sibling = flat + 1 - 2 * core

    def wrap(p):
        return lax.rem(p + 2 * SIDE, SIDE)

    def device(px, py):
        return (px * SIDE + py) * 2 + core

    loads = [
        pltpu.make_async_copy(kg, kgb.at[pl.ds(0, tokens)], load_sem.at[0]),
        pltpu.make_async_copy(weight, wb, load_sem.at[1]),
        pltpu.make_async_copy(adam_m, mb, load_sem.at[2]),
        pltpu.make_async_copy(adam_v, vb, load_sem.at[3]),
        pltpu.make_async_copy(anchor, ab, load_sem.at[4]),
        pltpu.make_async_copy(momentum, ob, load_sem.at[5]),
    ]

    def own_block(k):
        start = pl.multiple_of((2 * k + core) * 128, 128)
        return pltpu.make_async_copy(
            act.at[:, pl.ds(start, 128)], actb.at[k, pl.ds(0, tokens)], act_sem.at[k]
        )

    def sibling_block(k):
        start = pl.multiple_of((2 * k + 1 - core) * 128, 128)
        return pltpu.make_async_remote_copy(
            src_ref=act.at[:, pl.ds(start, 128)],
            dst_ref=actb.at[k, pl.ds(tokens, tokens)],
            send_sem=sib_send.at[k],
            recv_sem=sib_recv.at[k],
            device_id={"fsdp": sibling},
            device_id_type=MESH,
        )

    def sibling_kg(half):
        cols = slice(half * half_cols, (half + 1) * half_cols)
        return pltpu.make_async_remote_copy(
            src_ref=kg.at[:, cols],
            dst_ref=kgb.at[pl.ds(tokens, tokens), cols],
            send_sem=sib_send.at[SIDE * SIDE + half],
            recv_sem=sib_recv.at[SIDE * SIDE + half],
            device_id={"fsdp": sibling},
            device_id_type=MESH,
        )

    def far_x(visit):
        def one(e, carry):
            visit(wrap(x + 2) * SIDE + e)
            return carry

        lax.fori_loop(0, SIDE, one, 0)

    def far_y(visit):
        def one(e, carry):
            visit(wrap(x + 3 + e) * SIDE + wrap(y + 2))
            return carry

        lax.fori_loop(0, SIDE - 1, one, 0)

    def rest(visit):
        def one(e, carry):
            visit(wrap(x + 3 + lax.div(e, 3)) * SIDE + wrap(y + 3 + lax.rem(e, 3)))
            return carry

        lax.fori_loop(0, 9, one, 0)

    barrier = pltpu.get_barrier_semaphore()
    for peer in (
        sibling,
        device(wrap(x + 1), y),
        device(wrap(x - 1), y),
        device(x, wrap(y + 1)),
        device(x, wrap(y - 1)),
    ):
        pl.semaphore_signal(barrier, inc=1, device_id={"fsdp": peer}, device_id_type=MESH)

    def greet(d, carry):
        pl.semaphore_signal(
            barrier, inc=1, device_id={"island": lax.rem(me + d, islands)}, device_id_type=MESH
        )
        return carry

    lax.fori_loop(1, islands, greet, 0)
    pl.semaphore_wait(barrier, 5 + islands - 1)

    def both(k):
        sibling_block(k).start()
        own_block(k).start()

    sibling_kg(0).start()
    loads[0].start()
    far_x(both)
    sibling_kg(1).start()
    far_y(both)
    rest(both)
    for copy in loads[1:]:
        copy.start()

    def neighbour(axis, direction):
        sign = 1 - 2 * direction
        if axis == 0:
            return device(wrap(x + sign), y)
        return device(x, wrap(y + sign))

    def axis_of(phase, half):
        return phase ^ half

    def position(axis):
        return x if axis == 0 else y

    def piece(s, phase, half, group, section):
        if phase == 0:
            return part.at[s, half, pl.ds(group * SIDE + 2 * section, 2)]
        own = position(axis_of(0, half))
        rows = part.shape[3] // 2
        return part.at[s, half, own * SIDE + group, pl.ds(rows * section, rows)]

    def landing(s, phase, half, direction, message):
        buffer = got1 if phase == 0 else got2
        return buffer.at[s, half, direction, message]

    def send(s, phase, half, direction, message):
        axis = axis_of(phase, half)
        pos = position(axis)
        sign = 1 - 2 * direction
        group = wrap(pos + 2) if message == 0 else wrap(pos + sign)
        section = 1 - direction if message == 1 else direction
        return pltpu.make_async_remote_copy(
            src_ref=piece(s, phase, half, group, section),
            dst_ref=landing(s, phase, half, direction, message),
            send_sem=xy_send.at[s, phase],
            recv_sem=(
                xy_relay.at[s, phase, half, direction] if message == 0 else xy_last.at[s, phase, half]
            ),
            device_id={"fsdp": neighbour(axis, direction)},
            device_id_type=MESH,
        )

    def first(s, phase, half):
        for direction in (0, 1):
            send(s, phase, half, direction, 0).start()

    def second(s, phase, half):
        for direction in (0, 1):
            send(s, phase, half, direction, 1).start()

    def relay(s, phase, half):
        pos = position(axis_of(phase, half))
        for direction in (0, 1):
            send(s, phase, half, direction, 0).wait_recv()
            target = piece(s, phase, half, wrap(pos + 1 - 2 * direction), direction)
            target[...] += landing(s, phase, half, direction, 0)[...]
            send(s, phase, half, direction, 2).start()

    def arrived(s, phase, half):
        buffer = got1 if phase == 0 else got2
        landed = buffer.at[s, half, :, pl.ds(1, 2)]
        pltpu.make_async_copy(landed, landed, xy_last.at[s, phase, half]).wait()

    def collect(s, phase, half):
        arrived(s, phase, half)
        pos = position(axis_of(phase, half))
        for section in (0, 1):
            target = piece(s, phase, half, pos, section)
            target[...] += (
                landing(s, phase, half, section, 2)[...]
                + landing(s, phase, half, 1 - section, 1)[...]
            )

    def share_send(s, j):
        chunk, parity = s // PAIR, s % PAIR
        owner = PAIR * j + parity
        return pltpu.make_async_remote_copy(
            src_ref=step_b.at[s, j],
            dst_ref=zgot.at[chunk, me],
            send_sem=zr_send.at[chunk],
            recv_sem=zr_recv.at[chunk],
            device_id={"island": owner},
            device_id_type=MESH,
        )

    def all_of(chunk, sem):
        others = zgot.at[chunk, pl.ds(0, islands - 1)]
        return pltpu.make_async_copy(others, others, sem.at[chunk])

    def fresh_send(chunk, owner, target):
        return pltpu.make_async_remote_copy(
            src_ref=fresh.at[chunk],
            dst_ref=w_out.at[chunk, owner],
            send_sem=ag_send.at[chunk],
            recv_sem=ag_recv.at[chunk],
            device_id={"island": target},
            device_id_type=MESH,
        )

    save_moments = (
        pltpu.make_async_copy(mnb, m_out, out_sem.at[0]),
        pltpu.make_async_copy(vnb, v_out, out_sem.at[1]),
    )
    save_outer = (
        pltpu.make_async_copy(anb, a_out, out_sem.at[2]),
        pltpu.make_async_copy(onb, o_out, out_sem.at[3]),
        pltpu.make_async_copy(fresh, w_out.at[:, me], out_sem.at[4]),
    )

    def columns(chunk, half):
        return slice(half * half_cols + chunk * 128, half * half_cols + (chunk + 1) * 128)

    def inner_step(s):
        chunk, parity = s // PAIR, s % PAIR
        for half in (0, 1):
            arrived(s, 1, half)
            pos = position(axis_of(1, half))
            cols = columns(chunk, half)
            for section in (0, 1):
                js = slice(section * groups // 2, (section + 1) * groups // 2)
                grad = (
                    piece(s, 1, half, pos, section)[...]
                    + landing(s, 1, half, section, 2)[...]
                    + landing(s, 1, half, 1 - section, 1)[...]
                ).reshape(groups // 2, 8, 128)
                m_next = beta_first * mb[js, parity, :, cols] + (1.0 - beta_first) * grad
                v_next = beta_second * vb[js, parity, :, cols] + (1.0 - beta_second) * grad * grad
                old = wb[js, parity, :, cols]
                mnb[js, parity, :, cols] = m_next
                vnb[js, parity, :, cols] = v_next
                step_b[s, js, half] = old - inner_rate * (
                    m_next / (jnp.sqrt(v_next) + epsilon) + decay_rate * old
                )

        def one(k, carry):
            sign = 1 - 2 * lax.rem(k, 2)
            even = 2 * lax.div(k + 1, 2) * sign
            uneven = lax.rem(k, 2) * k - (1 - lax.rem(k, 2)) * (k + 1)
            off = lax.rem(me + parity, 2)
            owner = lax.rem(me + islands // 2 + even + off * (uneven - even) + islands, islands)

            @pl.when(owner != me)
            def _():
                share_send(s, lax.div(owner, PAIR)).start()

            return carry

        lax.fori_loop(0, groups, one, 0)

    def outer_step(s):
        chunk, parity = s // PAIR, s % PAIR

        @pl.when(lax.rem(me, PAIR) == parity)
        def _():
            zgot[chunk, me] = step_b[s, lax.div(me, PAIR)]
            all_of(chunk, zr_recv).wait()
            total = jnp.sum(zgot[chunk], axis=0)
            for half in (0, 1):
                cols = columns(chunk, half)
                old = ab[:, cols]
                shift = old - total[half] / float(islands)
                moment = outer_beta * ob[:, cols] + shift
                new = old - outer_rate * (shift + outer_beta * moment)
                fresh[chunk, half] = new
                anb[:, cols] = new
                onb[:, cols] = moment

            def one(k, carry):
                d = islands // 2 + lax.div(k + 1, 2) * (1 - 2 * lax.rem(k, 2))
                fresh_send(chunk, me, lax.rem(me + d, islands)).start()
                return carry

            lax.fori_loop(0, islands - 1, one, 0)

    def wait_block(k):
        own_block(k).wait()
        sibling_block(k).wait_recv()

    def multiply(half, offset):
        axis = axis_of(0, half)
        group = wrap(position(axis) + offset)

        blocks = [
            actb[group * SIDE + e if half == 0 else e * SIDE + group] for e in range(SIDE)
        ]
        product = lax.dot_general(
            jnp.concatenate(blocks, axis=1),
            kgb[:, half * half_cols : (half + 1) * half_cols],
            (((0,), (0,)), ((), ())),
            preferred_element_type=jnp.float32,
        )
        for e in range(SIDE):
            for s in range(STAGES):
                chunk, parity = s // PAIR, s % PAIR
                for j in range(groups):
                    row = (e * islands + PAIR * j + parity) * 8
                    part[s, half, group * SIDE + e, j * 8 : (j + 1) * 8, :] = product[
                        row : row + 8, chunk * 128 : (chunk + 1) * 128
                    ]

    early_first = (0, 1)
    early_second = (0, 1)
    loads[0].wait()
    sibling_kg(0).wait_recv()
    far_x(wait_block)
    multiply(0, 2)
    for s in early_first:
        first(s, 0, 0)
    sibling_kg(1).wait_recv()
    far_y(wait_block)
    multiply(1, 2)
    for s in early_first:
        first(s, 0, 1)
    rest(wait_block)
    for direction, offset in ((0, 1), (1, 3)):
        for half in (0, 1):
            multiply(half, offset)
            for s in early_second:
                send(s, 0, half, direction, 1).start()
    for half in (0, 1):
        multiply(half, 0)

    def firsts(s):
        for half in (0, 1):
            first(s, 0, half)

    def seconds(s):
        for half in (0, 1):
            second(s, 0, half)

    def relays_far(s):
        for half in (0, 1):
            relay(s, 0, half)

    def relays_near(s):
        for half in (0, 1):
            relay(s, 1, half)

    def collects(s):
        for half in (0, 1):
            collect(s, 0, half)
            first(s, 1, half)
            second(s, 1, half)

    relays_far(0)
    firsts(2)
    relays_far(1)
    seconds(2)
    collects(0)
    firsts(3)
    relays_far(2)
    collects(1)
    relays_near(0)
    seconds(3)
    relays_far(3)
    collects(2)
    relays_near(1)
    for copy in loads[1:]:
        copy.wait()
    inner_step(0)
    collects(3)
    relays_near(2)
    inner_step(1)
    relays_near(3)
    inner_step(2)
    inner_step(3)
    for copy in save_moments:
        copy.start()
    outer_step(0)
    outer_step(1)
    outer_step(2)
    outer_step(3)
    for copy in save_outer:
        copy.start()

    for half in (0, 1):
        sibling_kg(half).wait_send()
    for visits in (far_x, far_y, rest):
        visits(lambda k: sibling_block(k).wait_send())

    for s in range(STAGES):
        for phase, buffer in ((0, got1), (1, got2)):
            pltpu.make_async_copy(buffer.at[s], buffer.at[s], xy_send.at[s, phase]).wait()
    for chunk in (0, 1):
        all_of(chunk, zr_send).wait()
        all_of(chunk, ag_recv).wait()
    for chunk in (0, 1):
        all_of(chunk, ag_send).wait()
    for copy in save_moments + save_outer:
        copy.wait()


def place(m, v, w, a, o, m_out, v_out, w_out, a_out, o_out, sem):
    pairs = [(m, m_out), (v, v_out), (a, a_out), (o, o_out)]
    for half in (0, 1):
        for chunk in (0, 1):
            start = (2 * half + chunk) * 128
            pairs.append((w.at[chunk, :, half], w_out.at[:, :, start : start + 128]))
    copies = [pltpu.make_async_copy(old, new, sem.at[i]) for i, (old, new) in enumerate(pairs)]
    for copy in copies:
        copy.start()
    for copy in copies:
        copy.wait()


def shards(activations, key_grad, island_weight, adam_m, adam_v, anchor, outer_momentum):
    _, tokens, features = activations.shape
    columns = key_grad.shape[2]
    rows = island_weight.shape[1]
    islands = lax.axis_size("island")
    groups = islands // PAIR
    share = rows // islands
    blocks = SIDE * SIDE
    f32 = jnp.float32
    state = (groups, PAIR, share, columns)
    hbm = pl.BlockSpec(memory_space=pl.ANY)
    dma = pltpu.SemaphoreType.DMA
    stage_rows = rows // PAIR
    tiles = (2, share, 128)

    def kernel(*refs):
        window(islands, *refs)

    results = pl.pallas_call(
        kernel,
        out_shape=(
            jax.ShapeDtypeStruct(state, f32),
            jax.ShapeDtypeStruct(state, f32),
            jax.ShapeDtypeStruct((2, islands) + tiles, f32),
            jax.ShapeDtypeStruct((share, columns), f32),
            jax.ShapeDtypeStruct((share, columns), f32),
        ),
        in_specs=[hbm] * 7,
        out_specs=(hbm,) * 5,
        scratch_shapes=[
            pltpu.VMEM((blocks, 2 * tokens, features // (2 * blocks)), jnp.bfloat16),
            pltpu.VMEM((2 * tokens, columns), jnp.bfloat16),
            pltpu.VMEM((STAGES, 2, blocks, stage_rows, 128), f32),
            pltpu.VMEM((STAGES, 2, 2, 3, 2, stage_rows, 128), f32),
            pltpu.VMEM((STAGES, 2, 2, 3, stage_rows // 2, 128), f32),
            pltpu.VMEM(state, f32),
            pltpu.VMEM(state, f32),
            pltpu.VMEM(state, f32),
            pltpu.VMEM(state, f32),
            pltpu.VMEM(state, f32),
            pltpu.VMEM((STAGES, groups) + tiles, f32),
            pltpu.VMEM((2, islands) + tiles, f32),
            pltpu.VMEM((share, columns), f32),
            pltpu.VMEM((share, columns), f32),
            pltpu.VMEM((share, columns), f32),
            pltpu.VMEM((share, columns), f32),
            pltpu.VMEM((2,) + tiles, f32),
            dma((6,)),
            dma((blocks,)),
            dma((blocks + 2,)),
            dma((blocks + 2,)),
            dma((STAGES, 2)),
            dma((STAGES, 2, 2, 2)),
            dma((STAGES, 2, 2)),
            dma((2,)),
            dma((2,)),
            dma((2,)),
            dma((2,)),
            dma((5,)),
        ],
        compiler_params=pltpu.CompilerParams(
            collective_id=0, has_side_effects=True, vmem_limit_bytes=40 * 1024 * 1024
        ),
    )(
        *(pltpu.with_memory_space_constraint(r, pltpu.MemorySpace.HBM) for r in (activations[0],
        key_grad[0],
        island_weight.reshape(state),
        adam_m.reshape(state),
        adam_v.reshape(state),
        anchor[0],
        outer_momentum[0])),
    )
    m_next, v_next, refreshed, new_anchor, moment = pl.pallas_call(
        place,
        out_shape=tuple(
            jax.ShapeDtypeStruct(shape, f32)
            for shape in (state, state, (islands, share, columns), (share, columns), (share, columns))
        ),
        in_specs=[hbm] * 5,
        out_specs=(hbm,) * 5,
        scratch_shapes=[dma((8,))],
        compiler_params=pltpu.CompilerParams(vmem_limit_bytes=1024 * 1024),
    )(*results)
    return (
        m_next.reshape(island_weight.shape),
        v_next.reshape(island_weight.shape),
        refreshed.reshape(rows, columns),
        new_anchor[None],
        moment[None],
    )


def solution(mesh):
    spec = P("island", "fsdp", None)
    return jax.shard_map(
        shards,
        mesh=mesh,
        in_specs=(spec,) * 7,
        out_specs=(spec, spec, P("fsdp", None), spec, spec),
        check_vma=False,
    )
```

```python
import jax
import jax.numpy as jnp
from jax import lax
from jax.experimental import pallas as pl
from jax.experimental.pallas import tpu as pltpu
from jax.sharding import PartitionSpec as P

beta_first = 0.9
beta_second = 0.95
epsilon = 1e-08
inner_rate = 0.0004
decay_rate = 0.1
outer_beta = 0.9
outer_rate = 0.7

SIDE = 4
PAIR = 2
STAGES = 2 * PAIR
MESH = pl.DeviceIdType.MESH


def window(
    islands,
    act, kg, weight, adam_m, adam_v, anchor, momentum,
    m_out, v_out, w_out, a_out, o_out,
    actb, kgb, part, got1, got2, wb, mb, vb, mnb, vnb, step_b, zgot, ab, ob, anb, onb, fresh,
    load_sem, act_sem, sib_send, sib_recv, xy_send, xy_relay, xy_last, zr_send, zr_recv, ag_send, ag_recv, out_sem,
):
    me = lax.axis_index("island")
    flat = lax.axis_index("fsdp")
    core = lax.rem(flat, 2)
    chip = lax.div(flat, 2)
    x = lax.div(chip, SIDE)
    y = lax.rem(chip, SIDE)
    tokens = kg.shape[0]
    groups = islands // PAIR
    half_cols = kgb.shape[1] // 2
    sibling = flat + 1 - 2 * core

    def wrap(p):
        return lax.rem(p + 2 * SIDE, SIDE)

    def device(px, py):
        return (px * SIDE + py) * 2 + core

    loads = [
        pltpu.make_async_copy(kg, kgb.at[pl.ds(0, tokens)], load_sem.at[0]),
        pltpu.make_async_copy(weight, wb, load_sem.at[1]),
        pltpu.make_async_copy(adam_m, mb, load_sem.at[2]),
        pltpu.make_async_copy(adam_v, vb, load_sem.at[3]),
        pltpu.make_async_copy(anchor, ab, load_sem.at[4]),
        pltpu.make_async_copy(momentum, ob, load_sem.at[5]),
    ]

    def own_block(k):
        start = pl.multiple_of((2 * k + core) * 128, 128)
        return pltpu.make_async_copy(
            act.at[:, pl.ds(start, 128)], actb.at[k, pl.ds(0, tokens)], act_sem.at[k]
        )

    def sibling_block(k):
        start = pl.multiple_of((2 * k + 1 - core) * 128, 128)
        return pltpu.make_async_remote_copy(
            src_ref=act.at[:, pl.ds(start, 128)],
            dst_ref=actb.at[k, pl.ds(tokens, tokens)],
            send_sem=sib_send.at[k],
            recv_sem=sib_recv.at[k],
            device_id={"fsdp": sibling},
            device_id_type=MESH,
        )

    def sibling_kg(half):
        cols = slice(half * half_cols, (half + 1) * half_cols)
        return pltpu.make_async_remote_copy(
            src_ref=kg.at[:, cols],
            dst_ref=kgb.at[pl.ds(tokens, tokens), cols],
            send_sem=sib_send.at[SIDE * SIDE + half],
            recv_sem=sib_recv.at[SIDE * SIDE + half],
            device_id={"fsdp": sibling},
            device_id_type=MESH,
        )

    def far_x(visit):
        def one(e, carry):
            visit(wrap(x + 2) * SIDE + e)
            return carry

        lax.fori_loop(0, SIDE, one, 0)

    def far_y(visit):
        def one(e, carry):
            visit(wrap(x + 3 + e) * SIDE + wrap(y + 2))
            return carry

        lax.fori_loop(0, SIDE - 1, one, 0)

    def rest(visit):
        def one(e, carry):
            visit(wrap(x + 3 + lax.div(e, 3)) * SIDE + wrap(y + 3 + lax.rem(e, 3)))
            return carry

        lax.fori_loop(0, 9, one, 0)

    barrier = pltpu.get_barrier_semaphore()
    for peer in (
        sibling,
        device(wrap(x + 1), y),
        device(wrap(x - 1), y),
        device(x, wrap(y + 1)),
        device(x, wrap(y - 1)),
    ):
        pl.semaphore_signal(barrier, inc=1, device_id={"fsdp": peer}, device_id_type=MESH)

    def greet(d, carry):
        pl.semaphore_signal(
            barrier, inc=1, device_id={"island": lax.rem(me + d, islands)}, device_id_type=MESH
        )
        return carry

    lax.fori_loop(1, islands, greet, 0)
    pl.semaphore_wait(barrier, 5 + islands - 1)

    def both(k):
        sibling_block(k).start()
        own_block(k).start()

    sibling_kg(0).start()
    loads[0].start()
    far_x(both)
    sibling_kg(1).start()
    far_y(both)
    rest(both)
    for copy in loads[1:]:
        copy.start()

    def neighbour(axis, direction):
        sign = 1 - 2 * direction
        if axis == 0:
            return device(wrap(x + sign), y)
        return device(x, wrap(y + sign))

    def axis_of(phase, half):
        return phase ^ half

    def position(axis):
        return x if axis == 0 else y

    def piece(s, phase, half, group, section):
        if phase == 0:
            return part.at[s, half, pl.ds(group * SIDE + 2 * section, 2)]
        own = position(axis_of(0, half))
        rows = part.shape[3] // 2
        return part.at[s, half, own * SIDE + group, pl.ds(rows * section, rows)]

    def landing(s, phase, half, direction, message):
        buffer = got1 if phase == 0 else got2
        return buffer.at[s, half, direction, message]

    def send(s, phase, half, direction, message):
        axis = axis_of(phase, half)
        pos = position(axis)
        sign = 1 - 2 * direction
        group = wrap(pos + 2) if message == 0 else wrap(pos + sign)
        section = 1 - direction if message == 1 else direction
        return pltpu.make_async_remote_copy(
            src_ref=piece(s, phase, half, group, section),
            dst_ref=landing(s, phase, half, direction, message),
            send_sem=xy_send.at[s, phase],
            recv_sem=(
                xy_relay.at[s, phase, half, direction] if message == 0 else xy_last.at[s, phase, half]
            ),
            device_id={"fsdp": neighbour(axis, direction)},
            device_id_type=MESH,
        )

    def first(s, phase, half):
        for direction in (0, 1):
            send(s, phase, half, direction, 0).start()

    def second(s, phase, half):
        for direction in (0, 1):
            send(s, phase, half, direction, 1).start()

    def relay(s, phase, half):
        pos = position(axis_of(phase, half))
        for direction in (0, 1):
            send(s, phase, half, direction, 0).wait_recv()
            target = piece(s, phase, half, wrap(pos + 1 - 2 * direction), direction)
            target[...] += landing(s, phase, half, direction, 0)[...]
            send(s, phase, half, direction, 2).start()

    def arrived(s, phase, half):
        buffer = got1 if phase == 0 else got2
        landed = buffer.at[s, half, :, pl.ds(1, 2)]
        pltpu.make_async_copy(landed, landed, xy_last.at[s, phase, half]).wait()

    def collect(s, phase, half):
        arrived(s, phase, half)
        pos = position(axis_of(phase, half))
        for section in (0, 1):
            target = piece(s, phase, half, pos, section)
            target[...] += (
                landing(s, phase, half, section, 2)[...]
                + landing(s, phase, half, 1 - section, 1)[...]
            )

    def share_send(s, j):
        chunk, parity = s // PAIR, s % PAIR
        owner = PAIR * j + parity
        return pltpu.make_async_remote_copy(
            src_ref=step_b.at[s, j],
            dst_ref=zgot.at[chunk, me],
            send_sem=zr_send.at[chunk],
            recv_sem=zr_recv.at[chunk],
            device_id={"island": owner},
            device_id_type=MESH,
        )

    def all_of(chunk, sem):
        others = zgot.at[chunk, pl.ds(0, islands - 1)]
        return pltpu.make_async_copy(others, others, sem.at[chunk])

    def fresh_send(chunk, owner, target):
        return pltpu.make_async_remote_copy(
            src_ref=fresh.at[chunk],
            dst_ref=w_out.at[chunk, owner],
            send_sem=ag_send.at[chunk],
            recv_sem=ag_recv.at[chunk],
            device_id={"island": target},
            device_id_type=MESH,
        )

    save_moments = (
        pltpu.make_async_copy(mnb, m_out, out_sem.at[0]),
        pltpu.make_async_copy(vnb, v_out, out_sem.at[1]),
    )
    save_outer = (
        pltpu.make_async_copy(anb, a_out, out_sem.at[2]),
        pltpu.make_async_copy(onb, o_out, out_sem.at[3]),
        pltpu.make_async_copy(fresh, w_out.at[:, me], out_sem.at[4]),
    )

    def columns(chunk, half):
        return slice(half * half_cols + chunk * 128, half * half_cols + (chunk + 1) * 128)

    def inner_step(s):
        chunk, parity = s // PAIR, s % PAIR
        for half in (0, 1):
            arrived(s, 1, half)
            pos = position(axis_of(1, half))
            cols = columns(chunk, half)
            for section in (0, 1):
                js = slice(section * groups // 2, (section + 1) * groups // 2)
                grad = (
                    piece(s, 1, half, pos, section)[...]
                    + landing(s, 1, half, section, 2)[...]
                    + landing(s, 1, half, 1 - section, 1)[...]
                ).reshape(groups // 2, 8, 128)
                m_next = beta_first * mb[js, parity, :, cols] + (1.0 - beta_first) * grad
                v_next = beta_second * vb[js, parity, :, cols] + (1.0 - beta_second) * grad * grad
                old = wb[js, parity, :, cols]
                mnb[js, parity, :, cols] = m_next
                vnb[js, parity, :, cols] = v_next
                step_b[s, js, half] = old - inner_rate * (
                    m_next / (jnp.sqrt(v_next) + epsilon) + decay_rate * old
                )

        middle, off = islands // 2, lax.rem(me + parity, PAIR)
        for k in range(groups):
            even = middle + 2 * ((k + 1) // 2) * (1 - 2 * (k % 2))
            uneven = middle + (k if k % 2 else -k - 1)
            owner = lax.rem(me + even + off * (uneven - even), islands)
            if even == 0:

                @pl.when(off == 1)
                def _(owner=owner):
                    share_send(s, lax.div(owner, PAIR)).start()

            else:
                share_send(s, lax.div(owner, PAIR)).start()

    def outer_step(s):
        chunk, parity = s // PAIR, s % PAIR

        @pl.when(lax.rem(me, PAIR) == parity)
        def _():
            zgot[chunk, me] = step_b[s, lax.div(me, PAIR)]
            all_of(chunk, zr_recv).wait()
            total = jnp.sum(zgot[chunk], axis=0)
            for half in (0, 1):
                cols = columns(chunk, half)
                old = ab[:, cols]
                shift = old - total[half] / float(islands)
                moment = outer_beta * ob[:, cols] + shift
                new = old - outer_rate * (shift + outer_beta * moment)
                fresh[chunk, half] = new
                anb[:, cols] = new
                onb[:, cols] = moment

            for away in range(islands // 2, 0, -1):
                for d in sorted({away, islands - away}):
                    fresh_send(chunk, me, lax.rem(me + d, islands)).start()

    def wait_block(k):
        own_block(k).wait()
        sibling_block(k).wait_recv()

    def multiply(half, offset):
        axis = axis_of(0, half)
        group = wrap(position(axis) + offset)

        blocks = [
            actb[group * SIDE + e if half == 0 else e * SIDE + group] for e in range(SIDE)
        ]
        product = lax.dot_general(
            jnp.concatenate(blocks, axis=1),
            kgb[:, half * half_cols : (half + 1) * half_cols],
            (((0,), (0,)), ((), ())),
            preferred_element_type=jnp.float32,
        )
        for e in range(SIDE):
            for s in range(STAGES):
                chunk, parity = s // PAIR, s % PAIR
                for j in range(groups):
                    row = (e * islands + PAIR * j + parity) * 8
                    part[s, half, group * SIDE + e, j * 8 : (j + 1) * 8, :] = product[
                        row : row + 8, chunk * 128 : (chunk + 1) * 128
                    ]

    early_first = (0, 1)
    early_second = (0, 1)
    loads[0].wait()
    sibling_kg(0).wait_recv()
    far_x(wait_block)
    multiply(0, 2)
    for s in early_first:
        first(s, 0, 0)
    sibling_kg(1).wait_recv()
    far_y(wait_block)
    multiply(1, 2)
    for s in early_first:
        first(s, 0, 1)
    rest(wait_block)
    for direction, offset in ((0, 1), (1, 3)):
        for half in (0, 1):
            multiply(half, offset)
            for s in early_second:
                send(s, 0, half, direction, 1).start()
    for half in (0, 1):
        multiply(half, 0)

    def firsts(s):
        for half in (0, 1):
            first(s, 0, half)

    def seconds(s):
        for half in (0, 1):
            second(s, 0, half)

    def relays_far(s):
        for half in (0, 1):
            relay(s, 0, half)

    def relays_near(s):
        for half in (0, 1):
            relay(s, 1, half)

    def collects(s):
        for half in (0, 1):
            collect(s, 0, half)
            first(s, 1, half)
            second(s, 1, half)

    relays_far(0)
    firsts(2)
    relays_far(1)
    seconds(2)
    collects(0)
    firsts(3)
    relays_far(2)
    collects(1)
    relays_near(0)
    seconds(3)
    relays_far(3)
    collects(2)
    relays_near(1)
    for copy in loads[1:]:
        copy.wait()
    inner_step(0)
    collects(3)
    relays_near(2)
    inner_step(1)
    relays_near(3)
    inner_step(2)
    inner_step(3)
    for copy in save_moments:
        copy.start()
    outer_step(0)
    outer_step(1)
    outer_step(2)
    outer_step(3)
    for copy in save_outer:
        copy.start()

    for half in (0, 1):
        sibling_kg(half).wait_send()
    for visits in (far_x, far_y, rest):
        visits(lambda k: sibling_block(k).wait_send())

    for s in range(STAGES):
        for phase, buffer in ((0, got1), (1, got2)):
            pltpu.make_async_copy(buffer.at[s], buffer.at[s], xy_send.at[s, phase]).wait()
    for chunk in (0, 1):
        all_of(chunk, zr_send).wait()
        all_of(chunk, ag_recv).wait()
    for chunk in (0, 1):
        all_of(chunk, ag_send).wait()
    for copy in save_moments + save_outer:
        copy.wait()


def place(m, v, w, a, o, m_out, v_out, w_out, a_out, o_out, sem):
    pairs = [(m, m_out), (v, v_out), (a, a_out), (o, o_out)]
    for half in (0, 1):
        for chunk in (0, 1):
            start = (2 * half + chunk) * 128
            pairs.append((w.at[chunk, :, half], w_out.at[:, :, start : start + 128]))
    copies = [pltpu.make_async_copy(old, new, sem.at[i]) for i, (old, new) in enumerate(pairs)]
    for copy in copies:
        copy.start()
    for copy in copies:
        copy.wait()


def shards(activations, key_grad, island_weight, adam_m, adam_v, anchor, outer_momentum):
    _, tokens, features = activations.shape
    columns = key_grad.shape[2]
    rows = island_weight.shape[1]
    islands = lax.axis_size("island")
    groups = islands // PAIR
    share = rows // islands
    blocks = SIDE * SIDE
    f32 = jnp.float32
    state = (groups, PAIR, share, columns)
    hbm = pl.BlockSpec(memory_space=pl.ANY)
    dma = pltpu.SemaphoreType.DMA
    stage_rows = rows // PAIR
    tiles = (2, share, 128)

    def kernel(*refs):
        window(islands, *refs)

    results = pl.pallas_call(
        kernel,
        out_shape=(
            jax.ShapeDtypeStruct(state, f32),
            jax.ShapeDtypeStruct(state, f32),
            jax.ShapeDtypeStruct((2, islands) + tiles, f32),
            jax.ShapeDtypeStruct((share, columns), f32),
            jax.ShapeDtypeStruct((share, columns), f32),
        ),
        in_specs=[hbm] * 7,
        out_specs=(hbm,) * 5,
        scratch_shapes=[
            pltpu.VMEM((blocks, 2 * tokens, features // (2 * blocks)), jnp.bfloat16),
            pltpu.VMEM((2 * tokens, columns), jnp.bfloat16),
            pltpu.VMEM((STAGES, 2, blocks, stage_rows, 128), f32),
            pltpu.VMEM((STAGES, 2, 2, 3, 2, stage_rows, 128), f32),
            pltpu.VMEM((STAGES, 2, 2, 3, stage_rows // 2, 128), f32),
            pltpu.VMEM(state, f32),
            pltpu.VMEM(state, f32),
            pltpu.VMEM(state, f32),
            pltpu.VMEM(state, f32),
            pltpu.VMEM(state, f32),
            pltpu.VMEM((STAGES, groups) + tiles, f32),
            pltpu.VMEM((2, islands) + tiles, f32),
            pltpu.VMEM((share, columns), f32),
            pltpu.VMEM((share, columns), f32),
            pltpu.VMEM((share, columns), f32),
            pltpu.VMEM((share, columns), f32),
            pltpu.VMEM((2,) + tiles, f32),
            dma((6,)),
            dma((blocks,)),
            dma((blocks + 2,)),
            dma((blocks + 2,)),
            dma((STAGES, 2)),
            dma((STAGES, 2, 2, 2)),
            dma((STAGES, 2, 2)),
            dma((2,)),
            dma((2,)),
            dma((2,)),
            dma((2,)),
            dma((5,)),
        ],
        compiler_params=pltpu.CompilerParams(
            collective_id=0, has_side_effects=True, vmem_limit_bytes=40 * 1024 * 1024
        ),
    )(
        *(pltpu.with_memory_space_constraint(r, pltpu.MemorySpace.HBM) for r in (activations[0],
        key_grad[0],
        island_weight.reshape(state),
        adam_m.reshape(state),
        adam_v.reshape(state),
        anchor[0],
        outer_momentum[0])),
    )
    m_next, v_next, refreshed, new_anchor, moment = pl.pallas_call(
        place,
        out_shape=tuple(
            jax.ShapeDtypeStruct(shape, f32)
            for shape in (state, state, (islands, share, columns), (share, columns), (share, columns))
        ),
        in_specs=[hbm] * 5,
        out_specs=(hbm,) * 5,
        scratch_shapes=[dma((8,))],
        compiler_params=pltpu.CompilerParams(vmem_limit_bytes=1024 * 1024),
    )(*results)
    return (
        m_next.reshape(island_weight.shape),
        v_next.reshape(island_weight.shape),
        refreshed.reshape(rows, columns),
        new_anchor[None],
        moment[None],
    )


def solution(mesh):
    spec = P("island", "fsdp", None)
    return jax.shard_map(
        shards,
        mesh=mesh,
        in_specs=(spec,) * 7,
        out_specs=(spec, spec, P("fsdp", None), spec, spec),
        check_vma=False,
    )
```
